256 devices in a mesh: dom: 32 (over y_hi, z, core), col: 8 (over x, y_lo).
Axes of the slice: x: 4, y: 4 (y_hi: 2, y_lo: 2; y = y_hi * 2 + y_lo), z: 8, core: 2. Of those that a mesh axis runs over, the one named last changes fastest.
Arguments:
- tmat: bfloat16 [131072, 4096], P('dom', 'col'), may hold values from -6 to 6
- stored_mass_blocks: bfloat16 [8192, 128, 128], P('dom'), may hold values from -0.0007324219 to 0.0007324219
- block_index: int32 [8192, 2], P('dom'), may hold values from 0 to 35, as said below
- live_block_count: int32 [32], P('dom'), may hold values from 36 to 256, as said below
- send_rows: int32 [64, 256], P('dom'), may hold values from 0 to 4095, as said below
Outputs:
- reduced: float32 [512, 4096], P('dom', 'col')
The draws below stay inside these ranges and needn't reach their ends.
Inputs may be any that keep to these rules, and one draw needn't show every extreme that they name: `block_index`: row entries lie in 0 to 31 and column entries in 0 to 35. In each partition's list slot k < 32 is block (k, k), and slot 32 + m for m < 4 has block column 32 + m. `live_block_count`: some partition uses all 256 slots in every draw. `send_rows`: the 256 rows in each list are distinct local row numbers of the sending partition.
All inputs are finite; a program needn't handle non-finite values.
Results may differ from the reference program's by a relative error of at most 0.0029.
Values may be sent and summed in bfloat16 or wider, within the bound.
A program may use at most 128 MiB of HBM per device.

```python
import jax
import jax.numpy as jnp
from jax import lax

BS = 128
CB = 512
R_DEV = 4096
HB = 2
NBR = 32
NBLK = 256
HALO = 256
NROWS = 131072
KCOLS = 4096


def draw_block_index(key, part):
    parts = NROWS // R_DEV
    base = jax.random.fold_in(key, 11)
    key_one, key_two, key_three = jax.random.split(base, 3)
    extra = NBLK - NBR - 2 * HB
    rows_halo = jax.random.randint(key_one, (parts, 2 * HB), 0, NBR)
    additional_rows = jax.random.randint(key_two, (parts, extra), 0, NBR)
    cols_extra = jax.random.randint(key_three, (parts, extra), 0, NBR + 2 * HB)
    diag = jnp.broadcast_to(jnp.arange(NBR, dtype=jnp.int32)[None, :], (parts, NBR))
    halo_cols = jnp.broadcast_to((NBR + jnp.arange(2 * HB, dtype=jnp.int32))[None, :], (parts, 2 * HB))
    rows = jnp.concatenate([diag, rows_halo.astype(jnp.int32), additional_rows.astype(jnp.int32)], 1)
    cols = jnp.concatenate([diag, halo_cols, cols_extra.astype(jnp.int32)], 1)
    return jnp.stack([rows, cols], -1).reshape(parts * NBLK, 2).astype(jnp.int32)


def draw_live_block_count(key, part):
    parts = NROWS // R_DEV
    base = jax.random.fold_in(key, 23)
    key_one, key_two = jax.random.split(base)
    counts = jax.random.randint(key_one, (parts,), NBR + 2 * HB, NBLK + 1)
    chosen = jax.random.randint(key_two, (), 0, parts)
    counts = jnp.where(jnp.arange(parts) == chosen, NBLK, counts)
    return counts.astype(jnp.int32)


def draw_send_rows(key, part):
    parts = NROWS // R_DEV
    keys = jax.random.split(jax.random.fold_in(key, 37), 2 * parts)
    picked = jax.vmap(lambda k: jax.random.permutation(k, R_DEV)[:HALO])(keys)
    return picked.astype(jnp.int32)


def block_levels(key, dims, cuts, smallest, largest):
    def one(position, shards_of):
        steps = jax.random.uniform(jax.random.fold_in(jax.random.fold_in(key, 6), position), (shards_of,), jnp.float32, smallest / len(cuts), largest / len(cuts))
        return jnp.repeat(jnp.exp(steps), dims[position] // shards_of).reshape((-1,) + (1,) * (len(dims) - position - 1))

    level = one(*cuts[0])
    for cut in cuts[1:]:
        level = level * one(*cut)
    return level


def noise(stream_key, extent, scale, limit, shards=(), kind=jnp.bfloat16):
    drawn = jax.random.normal(stream_key, extent, jnp.float32) * scale
    if len(shards) > 0:
        drawn = block_levels(stream_key, extent, shards, -0.22, 0.18) * drawn
    return jnp.clip(drawn, min=-limit, max=limit).astype(kind)


def setup_inputs(seed: int = 0) -> dict:
    splits = jax.random.split(jax.random.key(seed), 6)
    tmat = noise(splits[0], (NROWS, KCOLS), 1.0, 6.0, ((0, 32), (1, 8)))
    stored_mass_blocks = noise(splits[1], (NROWS // BS * 8, BS, BS), (4 * BS * NROWS) ** -0.5, 0.0007324219, ((0, 32),))
    block_index = draw_block_index(jax.random.fold_in(splits[5], 71), 0)
    live_block_count = draw_live_block_count(jax.random.fold_in(splits[5], 71), 0)
    send_rows = draw_send_rows(jax.random.fold_in(splits[5], 71), 0)
    return dict(tmat=tmat, stored_mass_blocks=stored_mass_blocks, block_index=block_index, live_block_count=live_block_count, send_rows=send_rows)


def reference(tmat, stored_mass_blocks, block_index, live_block_count, send_rows):
    parts = NROWS // R_DEV
    panel = tmat[:, KCOLS - CB:]
    panel_parts = panel.reshape(parts, R_DEV, CB)
    sends = send_rows.reshape(parts, 2, HALO)
    picked = jax.vmap(lambda p, s: jnp.take(p, s, axis=0))(panel_parts, sends)
    zeros = jnp.zeros((1, HALO, CB), tmat.dtype)
    from_lower = jnp.concatenate([zeros, picked[:-1, 1]], 0)
    from_upper = jnp.concatenate([picked[1:, 0], zeros], 0)
    blocks = stored_mass_blocks.reshape(parts, NBLK, BS, BS)
    index = block_index.reshape(parts, NBLK, 2)
    tparts = tmat.reshape(parts, R_DEV, KCOLS)

    def one(acc, part):
        ext = jnp.concatenate([panel_parts[part], from_lower[part], from_upper[part]], 0)
        ext = ext.reshape(NBR + 2 * HB, BS, CB)
        sel = jnp.take(ext, index[part, :, 1], axis=0)
        prod = jnp.einsum("kab,kbw->kaw", blocks[part].astype(jnp.float32), sel.astype(jnp.float32),
                          precision=lax.Precision.HIGHEST)
        live_flags = jnp.arange(NBLK) < live_block_count[part]
        onehot = ((index[part, :, 0][None, :] == jnp.arange(NBR)[:, None]) & live_flags[None, :]).astype(jnp.float32)
        summed = jnp.einsum("rk,kaw->raw", onehot, prod, precision=lax.Precision.HIGHEST)
        interface_mass_panel = summed.reshape(R_DEV, CB).astype(jnp.bfloat16)
        term = lax.dot_general(interface_mass_panel, tparts[part], (((0,), (0,)), ((), ())),
                               preferred_element_type=jnp.float32)
        return acc + term, None

    total, _ = lax.scan(one, jnp.zeros((CB, KCOLS), jnp.float32), jnp.arange(parts))
    return total
```

```python
import functools

import jax
import jax.numpy as jnp
from jax import lax
from jax.experimental import pallas as pl
from jax.experimental.pallas import tpu as pltpu
from jax.sharding import PartitionSpec as P

F32 = jnp.float32
BF16 = jnp.bfloat16
BS = 128
W = 512
NB = 32
NS = 256
NPAIR = (NS + NB) // 2
NCH = 4
MC = W // NCH
OFF = 3
PER = 11

TREES = (
    ("00>10", "10>20", "20>21", "21>31", "10>11", "11>01", "20>30"),
    ("00>30", "30>20", "20>10", "30>31", "31>21", "21>11", "31>01"),
    ("00>01", "01>11", "11>21", "21>20", "01>31", "31>30", "11>10"),
)
FIRST = (0, 11, 22, 32)


def column_of(node):
    x, y = int(node[0]), int(node[1])
    return (x + 3) % 4 * 2 + 1 - y


def tree_tables():
    tables = []
    for edges in TREES:
        kids = [[-1, -1] for _ in range(8)]
        depth = [0] * 8
        for edge in edges:
            a, b = (column_of(n) for n in edge.split(">"))
            depth[b] = depth[a] + 1
            kids[a][0 if kids[a][0] < 0 else 1] = b
        tables.append((depth, [k[0] for k in kids], [k[1] for k in kids]))
    return tables


def pick(values, index):
    out = jnp.int32(values[0])
    for i, v in enumerate(values[1:], 1):
        out = jnp.where(index == i, jnp.int32(v), out)
    return out


def product_kernel(slot_ref, colm_ref, start_ref, tmat_ref, low_ref, up_ref, mass_ref, out_ref, ext, acc):
    eye = (
        lax.broadcasted_iota(jnp.int32, (BS, BS), 0) == lax.broadcasted_iota(jnp.int32, (BS, BS), 1)
    ).astype(BF16)

    def turn(block):
        parts = [
            lax.dot_general(
                eye, block[:, g * BS:(g + 1) * BS], (((1,), (1,)), ((), ())), preferred_element_type=F32
            ).astype(BF16)
            for g in range(W // BS)
        ]
        return jnp.concatenate(parts, axis=0)

    def turn_own(c, _):
        ext[c] = turn(tmat_ref[pl.ds(pl.multiple_of(c * BS, BS), BS), :])
        return 0

    lax.fori_loop(0, NB, turn_own, 0)
    for h in range(2):
        ext[NB + h] = turn(low_ref[h * BS:(h + 1) * BS, :])
        ext[NB + 2 + h] = turn(up_ref[h * BS:(h + 1) * BS, :])

    def row(r, _):
        def pair_product(q):
            lhs = jnp.concatenate([ext[colm_ref[2 * q]], ext[colm_ref[2 * q + 1]]], axis=1)
            rhs = jnp.concatenate([mass_ref[slot_ref[2 * q]], mass_ref[slot_ref[2 * q + 1]]], axis=1)
            return lax.dot_general(lhs, rhs, (((1,), (1,)), ((), ())), preferred_element_type=F32)

        begin = start_ref[r]
        acc[...] = pair_product(begin)

        def more(q, _):
            acc[...] += pair_product(q)
            return 0

        lax.fori_loop(begin + 1, start_ref[r + 1], more, 0)
        done = acc[...].astype(BF16).reshape(8, NCH, 16, BS)
        for j in range(NCH):
            out_ref[j, r] = done[:, j].reshape(MC, BS)
        return 0

    lax.fori_loop(0, NB, row, 0)


def mass_product(slot, colm, start, tmat, low, up, mass):
    smem = pl.BlockSpec(memory_space=pltpu.SMEM)
    vmem = pl.BlockSpec(memory_space=pltpu.VMEM)
    return pl.pallas_call(
        product_kernel,
        out_shape=jax.ShapeDtypeStruct((NCH, NB, MC, BS), BF16),
        in_specs=[smem] * 3 + [vmem] * 4,
        out_specs=vmem,
        scratch_shapes=[pltpu.VMEM((NB + 4, W, BS), BF16), pltpu.VMEM((W, BS), F32)],
        compiler_params=pltpu.CompilerParams(vmem_limit_bytes=48 << 20),
        name="mass_product",
    )(slot, colm, start, tmat, low, up, mass)


def couple_kernel(
    x_ref, tmat_hbm, out_ref, buf, tmat, accs, pairbuf, parts,
    load_sem, recv_sem, send_sem, pair_send, pair_recv, part_send, part_recv,
):
    col = lax.axis_index("col")
    dom = lax.axis_index("dom")
    core, zed, yhi = dom % 2, dom // 2 % 8, dom // 16
    chip = yhi * 8 + zed
    sibling = dom + 1 - 2 * core
    root = col == 7
    tables = tree_tables()
    depths = [pick(t[0], col) for t in tables]
    kids = [[pick(t[1], col), pick(t[2], col)] for t in tables]

    barrier = pltpu.get_barrier_semaphore()
    xpos, ylo = col // 2, col % 2
    for near in ((xpos + 1) % 4 * 2 + ylo, (xpos + 3) % 4 * 2 + ylo, xpos * 2 + 1 - ylo):
        pl.semaphore_signal(barrier, inc=1, device_id={"col": near})
    pl.semaphore_signal(barrier, inc=1, device_id={"dom": sibling})
    for step in range(1, 16):
        far = (chip + step) % 16
        pl.semaphore_signal(barrier, inc=1, device_id={"dom": far * 2 + core})
    tmat_load = pltpu.make_async_copy(tmat_hbm, tmat, load_sem.at[NCH])
    tmat_load.start()

    def own_load(j):
        return pltpu.make_async_copy(x_ref.at[j], buf.at[j], load_sem.at[j])

    @pl.when(root)
    def _():
        for j in range(NCH):
            own_load(j).start()

    pl.semaphore_wait(barrier, 19)

    def piece(t, s, j, b):
        return pltpu.make_async_remote_copy(
            src_ref=buf.at[j, b], dst_ref=buf.at[j, b],
            send_sem=send_sem.at[t, s], recv_sem=recv_sem.at[j, b],
            device_id={"col": kids[t][s]},
        )

    def contract(j, i):
        lhs = jnp.concatenate([buf[j, 4 * i + u] for u in range(4)], axis=1)
        rhs = tmat[pl.ds(pl.multiple_of(i * 512, 512), 512), :]
        accs[j] += jnp.dot(lhs, rhs, preferred_element_type=F32)

    def pair_copy(j):
        return pltpu.make_async_remote_copy(
            src_ref=accs.at[j], dst_ref=pairbuf.at[j // 2],
            send_sem=pair_send.at[j // 2], recv_sem=pair_recv.at[j // 2],
            device_id={"dom": sibling},
        )

    def part_copy(j, q):
        target = q // 4 * 16 + (q % 4 * 2 + j // 2) * 2 + core
        return target, pltpu.make_async_remote_copy(
            src_ref=accs.at[j, pl.ds(q * 16, 16)], dst_ref=parts.at[chip],
            send_sem=part_send.at[j // 2, q], recv_sem=part_recv.at[chip],
            device_id={"dom": target},
        )

    def hand_over(j):
        @pl.when(core != j % 2)
        def _():
            pair_copy(j).start()

    def spread(j):
        @pl.when(core == j % 2)
        def _():
            pair_copy(j).wait_recv()
            accs[j] += pairbuf[j // 2]
            for q in range(8):
                target, copy = part_copy(j, q)

                @pl.when(target != dom)
                def _():
                    copy.start()

                @pl.when(target == dom)
                def _():
                    parts[chip] = accs[j, q * 16:(q + 1) * 16]

    accs[...] = jnp.zeros_like(accs)

    def tick(k, _):
        @pl.when(root & (k < NCH * PER) & (k % PER == 0))
        def _():
            own_load(k // PER).wait()

        for t in range(3):
            p = k - OFF * depths[t]
            j, i = p // PER, p % PER
            b = FIRST[t] + i

            @pl.when((p >= 0) & (p < NCH * PER) & (i < FIRST[t + 1] - FIRST[t]))
            def _():
                @pl.when(depths[t] > 0)
                def _():
                    piece(t, 0, j, b).wait_recv()

                for s in range(2):
                    @pl.when(kids[t][s] >= 0)
                    def _():
                        piece(t, s, j, b).start()

        m = k - (PER + 4 * OFF)

        @pl.when(m == 0)
        def _():
            tmat_load.wait()

        @pl.when(m >= 0)
        def _():
            j, i = m // PER, m % PER

            @pl.when(i < 8)
            def _():
                contract(j, i)

            @pl.when(i == 8)
            def _():
                hand_over(j)

            @pl.when(i == 10)
            def _():
                spread(j)

        return 0

    lax.fori_loop(0, NCH * PER + 4 * OFF, tick, 0)
    last = NCH - 1
    lax.fori_loop(0, 8, lambda i, _: (contract(last, i), 0)[1], 0)
    hand_over(last)
    spread(last)

    for t in range(3):
        for s in range(2):
            @pl.when(kids[t][s] >= 0)
            def _():
                region = buf.at[:, pl.ds(FIRST[t], FIRST[t + 1] - FIRST[t])]
                pltpu.make_async_remote_copy(
                    src_ref=region, dst_ref=region, send_sem=send_sem.at[t, s],
                    recv_sem=recv_sem.at[0, 0], device_id={"col": kids[t][s]},
                ).wait_send()
    for j in range(NCH):
        @pl.when(core != j % 2)
        def _():
            pair_copy(j).wait_send()

        @pl.when(core == j % 2)
        def _():
            for q in range(8):
                target, copy = part_copy(j, q)

                @pl.when(target != dom)
                def _():
                    copy.wait_send()

    for step in range(1, 16):
        source = (chip + step) % 16
        pltpu.make_async_remote_copy(
            src_ref=parts.at[0], dst_ref=parts.at[source],
            send_sem=part_send.at[0, 0], recv_sem=part_recv.at[source],
            device_id={"dom": source * 2 + core},
        ).wait_recv()
    total = parts[0]
    for s in range(1, 16):
        total = total + parts[s]
    out_ref[...] = total


def couple(x, tmat):
    anyspace = pl.BlockSpec(memory_space=pl.ANY)
    return pl.pallas_call(
        couple_kernel,
        out_shape=jax.ShapeDtypeStruct((16, W), F32),
        in_specs=[anyspace, anyspace],
        out_specs=pl.BlockSpec(memory_space=pltpu.VMEM),
        scratch_shapes=[
            pltpu.VMEM((NCH, NB, MC, BS), BF16),
            pltpu.VMEM((NB * BS, W), BF16),
            pltpu.VMEM((NCH, MC, W), F32),
            pltpu.VMEM((2, MC, W), F32),
            pltpu.VMEM((16, 16, W), F32),
            pltpu.SemaphoreType.DMA((NCH + 1,)),
            pltpu.SemaphoreType.DMA((NCH, NB)),
            pltpu.SemaphoreType.DMA((3, 2)),
            pltpu.SemaphoreType.DMA((2,)),
            pltpu.SemaphoreType.DMA((2,)),
            pltpu.SemaphoreType.DMA((2, 8)),
            pltpu.SemaphoreType.DMA((16,)),
        ],
        compiler_params=pltpu.CompilerParams(
            collective_id=0, has_side_effects=True, vmem_limit_bytes=32 << 20
        ),
        name="couple",
    )(x, tmat)


def passed_along(block, axis, distance):
    devices = range(lax.axis_size(axis))
    route = [(i - distance, i) for i in devices if i - distance in devices]
    return lax.ppermute(block, axis, route)


def plan(block_index, live_block_count):
    slots = jnp.arange(NS, dtype=jnp.int32)
    key = jnp.where(slots < live_block_count[0], block_index[:, 0], NB)
    rows = jnp.arange(NB, dtype=jnp.int32)
    pairs = (jnp.sum((key[None, :] == rows[:, None]).astype(jnp.int32), axis=1) + 1) // 2
    edges = jnp.arange(NB + 1, dtype=jnp.int32)
    start = jnp.sum(jnp.where(rows[None, :] < edges[:, None], pairs[None, :], 0), axis=1)
    before = jnp.sum(((key[None, :] == key[:, None]) & (slots[None, :] < slots[:, None])).astype(jnp.int32), axis=1)
    base = jnp.sum(jnp.where(key[:, None] == edges[None, :], start[None, :], 0), axis=1)
    place = jnp.where(key < NB, 2 * base + before, 2 * NPAIR)
    hit = jnp.arange(2 * NPAIR, dtype=jnp.int32)[:, None] == place[None, :]
    slot = NS - jnp.sum(jnp.where(hit, NS - slots[None, :], 0), axis=1)
    colm = jnp.sum(jnp.where(hit, block_index[None, :, 1], 0), axis=1)
    return slot.astype(jnp.int32), colm.astype(jnp.int32), start.astype(jnp.int32)


def body(tmat, stored_mass_blocks, block_index, live_block_count, send_rows):
    slot, colm, start = plan(block_index, live_block_count)
    from_lower = passed_along(jnp.take(tmat, send_rows[1], axis=0), "dom", 1)
    from_upper = passed_along(jnp.take(tmat, send_rows[0], axis=0), "dom", -1)
    mass = jnp.concatenate([stored_mass_blocks, jnp.zeros((1, BS, BS), BF16)], 0)
    x = mass_product(slot, colm, start, tmat, from_lower, from_upper, mass)
    return couple(x, tmat)


def solution(mesh):
    return jax.shard_map(
        body,
        mesh=mesh,
        in_specs=(P("dom", "col"), P("dom", None, None), P("dom", None), P("dom"), P("dom", None)),
        out_specs=P("dom", "col"),
        check_vma=False,
    )
```

```python
import functools

import jax
import jax.numpy as jnp
from jax import lax
from jax.experimental import pallas as pl
from jax.experimental.pallas import tpu as pltpu
from jax.sharding import PartitionSpec as P

F32 = jnp.float32
BF16 = jnp.bfloat16
BS = 128
W = 512
NB = 32
NS = 256
NPAIR = (NS + NB) // 2
NCH = 4
MC = W // NCH
OFF = 6
PER = 11
RAW = 2
HALF = 256
UNR = 8

TREES = (
    ("00>10", "10>20", "20>21", "21>31", "10>11", "11>01", "20>30"),
    ("00>30", "30>20", "20>10", "30>31", "31>21", "21>11", "31>01"),
    ("00>01", "01>11", "11>21", "21>20", "01>31", "31>30", "11>10"),
)
FIRST = (0, 11, 22, 32)
HALO = (0, 3, 6, 8)
T_HALO = RAW * PER
T_MASS = T_HALO + 3
T_END = T_MASS + (NCH - RAW) * PER


def column_of(node):
    x, y = int(node[0]), int(node[1])
    return (x + 3) % 4 * 2 + 1 - y


def tree_tables():
    tables = []
    for edges in TREES:
        kids = [[-1, -1] for _ in range(8)]
        depth = [0] * 8
        for edge in edges:
            a, b = (column_of(n) for n in edge.split(">"))
            depth[b] = depth[a] + 1
            kids[a][0 if kids[a][0] < 0 else 1] = b
        tables.append((depth, [k[0] for k in kids], [k[1] for k in kids]))
    return tables


def pick(values, index):
    out = jnp.int32(values[0])
    for i, v in enumerate(values[1:], 1):
        out = jnp.where(index == i, jnp.int32(v), out)
    return out


def couple_kernel(
    slot_ref, colm_ref, keep_ref, last_ref, idx_ref, tmat_hbm, mass_hbm, out_ref,
    ext, xt, steps, acc, tmat, mass, perm, eye, lists, accs, pairbuf, parts,
    load_sem, halo_send, halo_recv, raw_recv, x_recv, send_sem,
    pair_send, pair_recv, part_send, part_recv,
):
    col = lax.axis_index("col")
    dom = lax.axis_index("dom")
    core, zed, yhi = dom % 2, dom // 2 % 8, dom // 16
    chip = yhi * 8 + zed
    sibling = dom + 1 - 2 * core
    root = col == 7
    tables = tree_tables()
    depths = [pick(t[0], col) for t in tables]
    kids = [[pick(t[1], col), pick(t[2], col)] for t in tables]

    def loop(n, f):
        def step(i, _):
            f(i)
            return 0

        lax.fori_loop(0, n, step, 0)

    tmat_load = pltpu.make_async_copy(tmat_hbm, tmat, load_sem.at[0])
    tmat_load.start()
    mass_load = pltpu.make_async_copy(mass_hbm, mass.at[pl.ds(0, NS)], load_sem.at[1])
    mass_load.start()

    barrier = pltpu.get_barrier_semaphore()
    xpos, ylo = col // 2, col % 2
    for near in ((xpos + 1) % 4 * 2 + ylo, (xpos + 3) % 4 * 2 + ylo, xpos * 2 + 1 - ylo):
        pl.semaphore_signal(barrier, inc=1, device_id={"col": near})
    for near in ((dom + 1) % 32, (dom + 31) % 32):
        pl.semaphore_signal(barrier, inc=1, device_id={"dom": near})

    def greet(step):
        far = (chip + step + 1) % 16
        pl.semaphore_signal(barrier, inc=1, device_id={"dom": far * 2 + core})

    loop(15, greet)

    mass[NS] = jnp.zeros((BS, BS), BF16)
    eye[...] = (
        lax.broadcasted_iota(jnp.int32, (HALF, HALF), 0) == lax.broadcasted_iota(jnp.int32, (HALF, HALF), 1)
    ).astype(BF16)

    def piece(kind, t, j, b, target, s):
        ref = ext.at[j, b] if kind < 2 else xt.at[RAW + j, b]
        sem = raw_recv.at[j, b] if kind < 2 else x_recv.at[j, b]
        return pltpu.make_async_remote_copy(
            src_ref=ref, dst_ref=ref, send_sem=send_sem.at[t, s, kind], recv_sem=sem,
            device_id={"col": target},
        )

    def mass_step(half, k):
        prods = []
        for u in range(UNR):
            q = k * UNR + u
            c1, c2 = colm_ref[2 * q], colm_ref[2 * q + 1]
            blocks = jnp.concatenate([mass[slot_ref[2 * q]], mass[slot_ref[2 * q + 1]]], axis=1)
            rows = jnp.concatenate(
                [jnp.concatenate([ext[2 * half, c], ext[2 * half + 1, c]], axis=1) for c in (c1, c2)], axis=0
            )
            prods.append(jnp.dot(blocks, rows, preferred_element_type=F32))
        total = acc[...]
        for u in range(UNR):
            total = total * keep_ref[k * UNR + u] + prods[u]
            steps[k * UNR + u] = total.astype(BF16)
        acc[...] = total

    def turn(half, r):
        done = lax.dot_general(
            eye[...], steps[last_ref[r]], (((1,), (1,)), ((), ())), preferred_element_type=F32
        ).astype(BF16)
        xt[2 * half, r] = done[:MC]
        xt[2 * half + 1, r] = done[MC:]

    def contract(j, i):
        lhs = jnp.concatenate([xt[j, 4 * i + u] for u in range(4)], axis=1)
        rhs = tmat[pl.ds(pl.multiple_of(i * 512, 512), 512), :]
        accs[j] += jnp.dot(lhs, rhs, preferred_element_type=F32)

    def pair_copy(j):
        return pltpu.make_async_remote_copy(
            src_ref=accs.at[j], dst_ref=pairbuf.at[j // 2],
            send_sem=pair_send.at[j // 2], recv_sem=pair_recv.at[j // 2],
            device_id={"dom": sibling},
        )

    def part_copy(j, q):
        target = q // 4 * 16 + (q % 4 * 2 + j // 2) * 2 + core
        return target, pltpu.make_async_remote_copy(
            src_ref=accs.at[j, pl.ds(pl.multiple_of(q * 16, 16), 16)], dst_ref=parts.at[chip],
            send_sem=part_send.at[j // 2, q], recv_sem=part_recv.at[chip],
            device_id={"dom": target},
        )

    def hand_over(j):
        @pl.when(core != j % 2)
        def _():
            pair_copy(j).start()

    def spread(j):
        @pl.when(core == j % 2)
        def _():
            pair_copy(j).wait_recv()
            accs[j] += pairbuf[j // 2]

            def send_part(q):
                target, copy = part_copy(j, q)

                @pl.when(target != dom)
                def _():
                    copy.start()

                @pl.when(target == dom)
                def _():
                    parts[chip] = accs[j, pl.ds(pl.multiple_of(q * 16, 16), 16)]

            loop(8, send_part)

    def from_root(kind, t, j, b):
        piece(kind, t, j, b, pick(tables[t][1], jnp.int32(7)), 0).start()

    @pl.when(root)
    def _():
        mode = lax.broadcasted_iota(jnp.int32, (W, W), 0)
        place = lax.broadcasted_iota(jnp.int32, (W, W), 1)
        wanted = (place // 16 % 8) * 64 + (place // MC) * 16 + place % 16
        perm[...] = (mode == wanted).astype(BF16)
        tmat_load.wait()
        pl.semaphore_wait(barrier, 20)

        def arrange(i):
            for t in range(3):
                b = FIRST[t] + i

                @pl.when(i < FIRST[t + 1] - FIRST[t])
                def _():
                    rows = tmat[pl.ds(pl.multiple_of(b * BS, BS), BS), :]
                    turned = jnp.dot(rows, perm[...], preferred_element_type=F32).astype(BF16)
                    for j in range(NCH):
                        ext[j, b] = turned[:, j * MC:(j + 1) * MC]
                    from_root(0, t, 0, b)

        loop(PER, arrange)

        def second(i):
            for t in range(3):
                @pl.when(i < FIRST[t + 1] - FIRST[t])
                def _():
                    from_root(0, t, 1, FIRST[t] + i)

        loop(PER, second)

        accs[...] = jnp.zeros_like(accs)

        def gather(k):
            lane = lax.broadcasted_iota(jnp.int32, (4 * BS, BS), 1)
            picks = jnp.concatenate(
                [(idx_ref[...] == lane + (k * 4 + u) * BS).astype(BF16) for u in range(4)], axis=1
            )
            rows = jnp.concatenate(
                [jnp.concatenate([ext[j, k * 4 + u] for j in range(NCH)], axis=1) for u in range(4)], axis=0
            )
            got = jnp.dot(picks, rows, preferred_element_type=F32)
            for h in range(4):
                accs[h] += got[h * BS:(h + 1) * BS]

        loop(NB // 4, gather)
        for h in range(4):
            got = accs[h].astype(BF16)
            for j in range(NCH):
                lists[j, h] = got[:, j * MC:(j + 1) * MC]

        def to_upper():
            return pltpu.make_async_remote_copy(
                src_ref=lists.at[:, pl.ds(2, 2)], dst_ref=ext.at[:, pl.ds(NB, 2)],
                send_sem=halo_send.at[0], recv_sem=halo_recv.at[0], device_id={"dom": (dom + 1) % 32},
            )

        def to_lower():
            return pltpu.make_async_remote_copy(
                src_ref=lists.at[:, pl.ds(0, 2)], dst_ref=ext.at[:, pl.ds(NB + 2, 2)],
                send_sem=halo_send.at[1], recv_sem=halo_recv.at[1], device_id={"dom": (dom + 31) % 32},
            )

        @pl.when(dom < 31)
        def _():
            to_upper().start()

        @pl.when(dom > 0)
        def _():
            to_lower().start()

        mass_load.wait()

        @pl.when(dom > 0)
        def _():
            to_upper().wait_recv()

        @pl.when(dom == 0)
        def _():
            ext[:, NB:NB + 2] = jnp.zeros((NCH, 2, BS, MC), BF16)

        @pl.when(dom < 31)
        def _():
            to_lower().wait_recv()

        @pl.when(dom == 31)
        def _():
            ext[:, NB + 2:NB + 4] = jnp.zeros((NCH, 2, BS, MC), BF16)

        for t in range(3):
            for h in range(HALO[t], HALO[t + 1]):
                from_root(1, t, h // 4, NB + h % 4)

        def half_product(turn_number):
            half = 1 - turn_number
            acc[...] = jnp.zeros_like(acc)
            loop(NPAIR // UNR, functools.partial(mass_step, half))

            def turn_send(i):
                for t in range(3):
                    @pl.when(i < FIRST[t + 1] - FIRST[t])
                    def _():
                        turn(half, FIRST[t] + i)

                        @pl.when(half == 1)
                        def _():
                            from_root(2, t, 0, FIRST[t] + i)

            loop(PER, turn_send)

            @pl.when(half == 1)
            def _():
                def send_last(i):
                    for t in range(3):
                        @pl.when(i < FIRST[t + 1] - FIRST[t])
                        def _():
                            from_root(2, t, 1, FIRST[t] + i)

                loop(PER, send_last)

        loop(2, half_product)
        accs[...] = jnp.zeros_like(accs)

        def reduce_chunk(j):
            loop(8, functools.partial(contract, j))
            hand_over(j)

            @pl.when(j > 0)
            def _():
                spread(j - 1)

        loop(NCH - 1, reduce_chunk)
        spread(NCH - 2)

        @pl.when(dom < 31)
        def _():
            to_upper().wait_send()

        @pl.when(dom > 0)
        def _():
            to_lower().wait_send()

    def relay(kind, t, j, b):
        piece(kind, t, j, b, kids[t][0], 0).wait_recv()
        for s in range(2):
            @pl.when(kids[t][s] >= 0)
            def _():
                piece(kind, t, j, b, kids[t][s], s).start()

    @pl.when(jnp.logical_not(root))
    def _():
        accs[...] = jnp.zeros_like(accs)
        acc[...] = jnp.zeros_like(acc)
        pl.semaphore_wait(barrier, 20)

        def tick(k):
            for t in range(3):
                p = k - OFF * depths[t]
                count = FIRST[t + 1] - FIRST[t]

                @pl.when((p >= 0) & (p < T_HALO) & (p % PER < count))
                def _():
                    relay(0, t, p // PER, FIRST[t] + p % PER)

                h = HALO[t] + p - T_HALO

                @pl.when((p >= T_HALO) & (h < HALO[t + 1]))
                def _():
                    relay(1, t, h // 4, NB + h % 4)

                x = p - T_MASS

                @pl.when((x >= 0) & (p < T_END) & (x % PER < count))
                def _():
                    relay(2, t, x // PER, FIRST[t] + x % PER)

            m = k - (T_MASS + 4 * OFF)

            @pl.when(m == 0)
            def _():
                tmat_load.wait()
                mass_load.wait()

            @pl.when((m >= 0) & (m < 9))
            def _():
                loop(2, lambda u: mass_step(0, 2 * m + u))

            @pl.when((m >= 9) & (m < 13))
            def _():
                i = m - 9
                for u in range(8):
                    turn(0, i * 8 + u)
                loop(4, lambda u: contract(u // 2, 2 * i + u % 2))

            @pl.when(m == 13)
            def _():
                hand_over(0)
                hand_over(1)

            @pl.when((m >= 14) & (m < 18))
            def _():
                loop(2, lambda u: contract(2, 2 * (m - 14) + u))

            @pl.when(m == 16)
            def _():
                loop(RAW, spread)

            @pl.when(m == 18)
            def _():
                hand_over(2)

            @pl.when(m == 21)
            def _():
                spread(2)

        loop(T_END + 4 * OFF, tick)

    last = NCH - 1
    loop(8, functools.partial(contract, last))
    hand_over(last)
    spread(last)

    for t in range(3):
        for s in range(2):
            @pl.when(kids[t][s] >= 0)
            def _():
                count = FIRST[t + 1] - FIRST[t]
                for kind, region in (
                    (0, ext.at[pl.ds(0, RAW), pl.ds(FIRST[t], count)]),
                    (1, ext.at[0, pl.ds(NB, HALO[t + 1] - HALO[t])]),
                    (2, xt.at[pl.ds(RAW, NCH - RAW), pl.ds(FIRST[t], count)]),
                ):
                    pltpu.make_async_remote_copy(
                        src_ref=region, dst_ref=region, send_sem=send_sem.at[t, s, kind],
                        recv_sem=raw_recv.at[0, 0], device_id={"col": kids[t][s]},
                    ).wait_send()
    def finish(j):
        @pl.when(core != j % 2)
        def _():
            pair_copy(j).wait_send()

        @pl.when(core == j % 2)
        def _():
            def sent(q):
                target, copy = part_copy(j, q)

                @pl.when(target != dom)
                def _():
                    copy.wait_send()

            loop(8, sent)

    loop(NCH, finish)

    def arrived(step):
        source = (chip + step + 1) % 16
        pltpu.make_async_remote_copy(
            src_ref=parts.at[0], dst_ref=parts.at[source],
            send_sem=part_send.at[0, 0], recv_sem=part_recv.at[source],
            device_id={"dom": source * 2 + core},
        ).wait_recv()

    loop(15, arrived)
    total = parts[0]
    for s in range(1, 16):
        total = total + parts[s]
    out_ref[...] = total


def couple(slot, colm, keep, last, idx, tmat, mass):
    smem = pl.BlockSpec(memory_space=pltpu.SMEM)
    vmem = pl.BlockSpec(memory_space=pltpu.VMEM)
    anyspace = pl.BlockSpec(memory_space=pl.ANY)
    dma = pltpu.SemaphoreType.DMA
    return pl.pallas_call(
        couple_kernel,
        out_shape=jax.ShapeDtypeStruct((16, W), F32),
        in_specs=[smem] * 4 + [vmem, anyspace, anyspace],
        out_specs=vmem,
        scratch_shapes=[
            pltpu.VMEM((NCH, NB + 4, BS, MC), BF16),
            pltpu.VMEM((NCH, NB, MC, BS), BF16),
            pltpu.VMEM((NPAIR, BS, HALF), BF16),
            pltpu.VMEM((BS, HALF), F32),
            pltpu.VMEM((NB * BS, W), BF16),
            pltpu.VMEM((NS + 1, BS, BS), BF16),
            pltpu.VMEM((W, W), BF16),
            pltpu.VMEM((HALF, HALF), BF16),
            pltpu.VMEM((NCH, 4, BS, MC), BF16),
            pltpu.VMEM((NCH, MC, W), F32),
            pltpu.VMEM((2, MC, W), F32),
            pltpu.VMEM((16, 16, W), F32),
            dma((2,)), dma((2,)), dma((2,)), dma((RAW, NB + 4)), dma((NCH - RAW, NB)), dma((3, 2, 3)),
            dma((2,)), dma((2,)), dma((2, 8)), dma((16,)),
        ],
        compiler_params=pltpu.CompilerParams(
            collective_id=0, has_side_effects=True, vmem_limit_bytes=60 << 20
        ),
        name="couple",
    )(slot, colm, keep, last, idx, tmat, mass)


def plan(block_index, live_block_count):
    slots = jnp.arange(NS, dtype=jnp.int32)
    key = jnp.where(slots < live_block_count[0], block_index[:, 0], NB)
    rows = jnp.arange(NB, dtype=jnp.int32)
    pairs = (jnp.sum((key[None, :] == rows[:, None]).astype(jnp.int32), axis=1) + 1) // 2
    edges = jnp.arange(NB + 1, dtype=jnp.int32)
    start = jnp.sum(jnp.where(rows[None, :] < edges[:, None], pairs[None, :], 0), axis=1)
    before = jnp.sum(((key[None, :] == key[:, None]) & (slots[None, :] < slots[:, None])).astype(jnp.int32), axis=1)
    base = jnp.sum(jnp.where(key[:, None] == edges[None, :], start[None, :], 0), axis=1)
    place = jnp.where(key < NB, 2 * base + before, 2 * NPAIR)
    hit = jnp.arange(2 * NPAIR, dtype=jnp.int32)[:, None] == place[None, :]
    slot = NS - jnp.sum(jnp.where(hit, NS - slots[None, :], 0), axis=1)
    colm = jnp.sum(jnp.where(hit, block_index[None, :, 1], 0), axis=1)
    opens = jnp.any(jnp.arange(NPAIR, dtype=jnp.int32)[:, None] == start[None, :NB], axis=1)
    keep = 1.0 - opens.astype(F32)
    last = start[1:] - 1
    return slot.astype(jnp.int32), colm.astype(jnp.int32), keep, last.astype(jnp.int32)


def body(tmat, stored_mass_blocks, block_index, live_block_count, send_rows):
    slot, colm, keep, last = plan(block_index, live_block_count)
    idx = jnp.broadcast_to(send_rows.reshape(4 * BS, 1), (4 * BS, BS))
    return couple(slot, colm, keep, last, idx, tmat, stored_mass_blocks)


def solution(mesh):
    return jax.shard_map(
        body,
        mesh=mesh,
        in_specs=(P("dom", "col"), P("dom", None, None), P("dom", None), P("dom"), P("dom", None)),
        out_specs=P("dom", "col"),
        check_vma=False,
    )
```

```python
import functools

import jax
import jax.numpy as jnp
from jax import lax
from jax.experimental import pallas as pl
from jax.experimental.pallas import tpu as pltpu
from jax.sharding import PartitionSpec as P

F32 = jnp.float32
BF16 = jnp.bfloat16
BS = 128
W = 512
NB = 32
NS = 256
NPAIR = (NS + NB) // 2
NCH = 4
MC = W // NCH
OFF = 5
PER = 11
RAW = 1
HALF = 256
LIST = 384

TREES = (
    ("00>10", "10>20", "20>21", "21>31", "10>11", "11>01", "20>30"),
    ("00>30", "30>20", "20>10", "30>31", "31>21", "21>11", "31>01"),
    ("00>01", "01>11", "11>21", "21>20", "01>31", "31>30", "11>10"),
)
FIRST = (0, 11, 22, 32)
HALO = (0, 2, 3, 4)
T_HALO = RAW * PER
T_MASS = T_HALO + 2
T_END = T_MASS + (NCH - RAW) * PER


def column_of(node):
    x, y = int(node[0]), int(node[1])
    return (x + 3) % 4 * 2 + 1 - y


def tree_tables():
    tables = []
    for edges in TREES:
        kids = [[-1, -1] for _ in range(8)]
        depth = [0] * 8
        for edge in edges:
            a, b = (column_of(n) for n in edge.split(">"))
            depth[b] = depth[a] + 1
            kids[a][0 if kids[a][0] < 0 else 1] = b
        tables.append((depth, [k[0] for k in kids], [k[1] for k in kids]))
    return tables


def pick(values, index):
    out = jnp.int32(values[0])
    for i, v in enumerate(values[1:], 1):
        out = jnp.where(index == i, jnp.int32(v), out)
    return out


def couple_kernel(
    live_ref, index_ref, shared_ref, tmat_hbm, mass_hbm, out_ref,
    order_v, order, ext, xt, steps, acc, tmat, mass, perm, eye, lists, accs, pairbuf, parts,
    load_sem, halo_send, halo_recv, raw_recv, x_recv, send_sem,
    pair_send, pair_recv, part_send, part_recv,
):
    col = lax.axis_index("col")
    dom = lax.axis_index("dom")
    core, zed, yhi = dom % 2, dom // 2 % 8, dom // 16
    chip = yhi * 8 + zed
    sibling = dom + 1 - 2 * core
    root = col == 7
    tables = tree_tables()
    depths = [pick(t[0], col) for t in tables]
    kids = [[pick(t[1], col), pick(t[2], col)] for t in tables]

    def loop(n, f):
        def step(i, _):
            f(i)
            return 0

        lax.fori_loop(0, n, step, 0)

    tmat_load = pltpu.make_async_copy(tmat_hbm, tmat, load_sem.at[0])
    tmat_load.start()
    mass_load = pltpu.make_async_copy(mass_hbm, mass.at[pl.ds(0, NS)], load_sem.at[1])

    barrier = pltpu.get_barrier_semaphore()
    xpos, ylo = col // 2, col % 2
    for near in ((xpos + 1) % 4 * 2 + ylo, (xpos + 3) % 4 * 2 + ylo, xpos * 2 + 1 - ylo):
        pl.semaphore_signal(barrier, inc=1, device_id={"col": near})
    for near in ((dom + 1) % 32, (dom + 31) % 32):
        pl.semaphore_signal(barrier, inc=1, device_id={"dom": near})

    def greet(step):
        far = (chip + step + 1) % 16
        pl.semaphore_signal(barrier, inc=1, device_id={"dom": far * 2 + core})

    loop(15, greet)

    mass[NS] = jnp.zeros((BS, BS), BF16)
    eye[...] = (
        lax.broadcasted_iota(jnp.int32, (HALF, HALF), 0) == lax.broadcasted_iota(jnp.int32, (HALF, HALF), 1)
    ).astype(BF16)

    def piece(kind, t, j, b, target, s):
        ref = ext.at[j, b] if kind < 2 else xt.at[RAW + j, b]
        sem = raw_recv.at[j, b] if kind < 2 else x_recv.at[j, b]
        return pltpu.make_async_remote_copy(
            src_ref=ref, dst_ref=ref, send_sem=send_sem.at[t, s, kind], recv_sem=sem,
            device_id={"col": target},
        )

    def plan():
        I32 = jnp.int32

        def iota(shape, axis):
            return lax.broadcasted_iota(I32, shape, axis)

        def add(condition, values, axis):
            return jnp.sum(jnp.where(condition, values, 0), axis=axis, keepdims=True)

        down = iota((NS, 1), 0)
        key = jnp.where(down < live_ref[0], index_ref[:, 0:1], NB)
        key_lane = add(iota((NS, NS), 0) == iota((NS, NS), 1), key, 0)
        before = add((key == key_lane) & (iota((NS, NS), 1) < iota((NS, NS), 0)), 1, 1)
        pairs_lane = (add(key == iota((NS, BS), 1), 1, 0) + 1) // 2
        pairs = (add(iota((NB, NS), 0) == key_lane, 1, 1) + 1) // 2
        base = add(iota((NS, BS), 1) < key, pairs_lane, 1)
        start = add(iota((NB, BS), 1) < iota((NB, BS), 0), pairs_lane, 1)
        place = jnp.where(key < NB, 2 * base + before, LIST)
        hit = place == iota((NS, LIST), 1)
        order_v[...] = jnp.zeros_like(order_v)
        order_v[0:1] = jnp.clip(NS - add(hit, NS - down, 0), 0, NS)
        order_v[1:2] = jnp.clip(add(hit, index_ref[:, 1:2], 0), 0, NB + 3)
        order_v[2:3] = 1 - add(start == iota((NB, LIST), 1), 1, 0)
        order_v[3:4] = jnp.clip(add(iota((NB, LIST), 0) <= iota((NB, LIST), 1), pairs, 0) - 1, 0, NPAIR - 1)
        copy = pltpu.make_async_copy(order_v, order, load_sem.at[2])
        copy.start()
        copy.wait()

    def mass_step(n, first, unr, k):
        prods = []
        for u in range(unr):
            q = k * unr + u
            blocks = jnp.concatenate([mass[order[0, 2 * q]], mass[order[0, 2 * q + 1]]], axis=1)
            rows = jnp.concatenate(
                [
                    jnp.concatenate([ext[first + v, order[1, 2 * q + w]] for v in range(n)], axis=1)
                    for w in range(2)
                ],
                axis=0,
            )
            prods.append(jnp.dot(blocks, rows, preferred_element_type=F32))
        total = acc[:, :n * MC]
        for u in range(unr):
            total = total * order[2, k * unr + u].astype(F32) + prods[u]
            steps[k * unr + u, :, :n * MC] = total.astype(BF16)
        acc[:, :n * MC] = total

    def turn(n, first, r):
        done = lax.dot_general(
            eye[:n * MC, :n * MC], steps[order[3, r], :, :n * MC], (((1,), (1,)), ((), ())),
            preferred_element_type=F32,
        ).astype(BF16)
        for v in range(n):
            xt[first + v, r] = done[v * MC:(v + 1) * MC]

    def contract(j, i):
        lhs = jnp.concatenate([xt[j, 4 * i + u] for u in range(4)], axis=1)
        rhs = tmat[pl.ds(pl.multiple_of(i * 512, 512), 512), :]
        accs[j] += jnp.dot(lhs, rhs, preferred_element_type=F32)

    def pair_copy(j):
        return pltpu.make_async_remote_copy(
            src_ref=accs.at[j], dst_ref=pairbuf.at[j // 2],
            send_sem=pair_send.at[j // 2], recv_sem=pair_recv.at[j // 2],
            device_id={"dom": sibling},
        )

    def part_copy(j, q):
        target = q // 4 * 16 + (q % 4 * 2 + j // 2) * 2 + core
        return target, pltpu.make_async_remote_copy(
            src_ref=accs.at[j, pl.ds(pl.multiple_of(q * 16, 16), 16)], dst_ref=parts.at[chip],
            send_sem=part_send.at[j // 2, q], recv_sem=part_recv.at[chip],
            device_id={"dom": target},
        )

    def hand_over(j):
        @pl.when(core != j % 2)
        def _():
            pair_copy(j).start()

    def spread(j):
        @pl.when(core == j % 2)
        def _():
            pair_copy(j).wait_recv()
            accs[j] += pairbuf[j // 2]

            def send_part(q):
                target, copy = part_copy(j, q)

                @pl.when(target != dom)
                def _():
                    copy.start()

                @pl.when(target == dom)
                def _():
                    parts[chip] = accs[j, pl.ds(pl.multiple_of(q * 16, 16), 16)]

            loop(8, send_part)

    def from_root(kind, t, j, b):
        piece(kind, t, j, b, pick(tables[t][1], jnp.int32(7)), 0).start()

    @pl.when(root)
    def _():
        mode = lax.broadcasted_iota(jnp.int32, (W, W), 0)
        place = lax.broadcasted_iota(jnp.int32, (W, W), 1)
        wanted = (place // 16 % 8) * 64 + (place // MC) * 16 + place % 16
        perm[...] = (mode == wanted).astype(BF16)
        plan()
        tmat_load.wait()
        mass_load.start()

        square = (2 * BS, 2 * BS)
        diagonal = lax.broadcasted_iota(jnp.int32, square, 0) == lax.broadcasted_iota(jnp.int32, square, 1)
        wanted_rows = [
            jnp.sum(jnp.where(diagonal, shared_ref[h:h + 1], 0), axis=1, keepdims=True) for h in range(2)
        ]
        idx = jnp.concatenate(wanted_rows, axis=0)
        accs[...] = jnp.zeros_like(accs)

        def gather(k):
            lane = lax.broadcasted_iota(jnp.int32, (4 * BS, 8 * BS), 1)
            picks = (idx == lane + k * 8 * BS).astype(BF16)
            rows = tmat[pl.ds(pl.multiple_of(k * 8 * BS, 8 * BS), 8 * BS), :]
            got = jnp.dot(picks, rows, preferred_element_type=F32)
            for h in range(4):
                accs[h] += got[h * BS:(h + 1) * BS]

        loop(NB // 8, gather)
        for h in range(4):
            got = jnp.dot(accs[h].astype(BF16), perm[...], preferred_element_type=F32).astype(BF16)
            for j in range(NCH):
                lists[j, h] = got[:, j * MC:(j + 1) * MC]

        pl.semaphore_wait(barrier, 20)
        def to_upper():
            return pltpu.make_async_remote_copy(
                src_ref=lists.at[:, pl.ds(2, 2)], dst_ref=ext.at[:, pl.ds(NB, 2)],
                send_sem=halo_send.at[0], recv_sem=halo_recv.at[0], device_id={"dom": (dom + 1) % 32},
            )

        def to_lower():
            return pltpu.make_async_remote_copy(
                src_ref=lists.at[:, pl.ds(0, 2)], dst_ref=ext.at[:, pl.ds(NB + 2, 2)],
                send_sem=halo_send.at[1], recv_sem=halo_recv.at[1], device_id={"dom": (dom + 31) % 32},
            )

        @pl.when(dom < 31)
        def _():
            to_upper().start()

        @pl.when(dom > 0)
        def _():
            to_lower().start()

        def arrange(n, first, b):
            rows = tmat[pl.ds(pl.multiple_of(b * BS, BS), BS), :]
            turned = jnp.dot(rows, perm[:, first * MC:(first + n) * MC], preferred_element_type=F32).astype(BF16)
            for v in range(n):
                ext[first + v, b] = turned[:, v * MC:(v + 1) * MC]

        def send_raw(i):
            for t in range(3):
                @pl.when(i < FIRST[t + 1] - FIRST[t])
                def _():
                    arrange(1, 0, FIRST[t] + i)
                    from_root(0, t, 0, FIRST[t] + i)

        def arrange_four(n, first, i):
            for u in range(4):
                arrange(n, first, 4 * i + u)

        loop(PER, send_raw)
        loop(NB // 4, functools.partial(arrange_four, 1, 1))
        mass_load.wait()

        @pl.when(dom > 0)
        def _():
            to_upper().wait_recv()

        @pl.when(dom == 0)
        def _():
            ext[:, NB:NB + 2] = jnp.zeros((NCH, 2, BS, MC), BF16)

        @pl.when(dom < 31)
        def _():
            to_lower().wait_recv()

        @pl.when(dom == 31)
        def _():
            ext[:, NB + 2:NB + 4] = jnp.zeros((NCH, 2, BS, MC), BF16)

        for t in range(3):
            for h in range(HALO[t], HALO[t + 1]):
                from_root(1, t, h // 4, NB + h % 4)

        def product(n, first, unr):
            acc[...] = jnp.zeros_like(acc)
            loop(NPAIR // unr, functools.partial(mass_step, n, first, unr))

        def send_mass(n, first, j, i):
            for t in range(3):
                @pl.when(i < FIRST[t + 1] - FIRST[t])
                def _():
                    if n:
                        turn(n, first, FIRST[t] + i)
                    from_root(2, t, j, FIRST[t] + i)

        product(1, 1, 16)
        loop(PER, functools.partial(send_mass, 1, 1, 0))
        loop(NB // 4, functools.partial(arrange_four, 2, 2))
        product(2, 2, 8)
        loop(PER, functools.partial(send_mass, 2, 2, 1))
        loop(PER, functools.partial(send_mass, 0, 2, 2))
        product(1, 0, 16)
        loop(NB, functools.partial(turn, 1, 0))
        accs[...] = jnp.zeros_like(accs)

        def reduce_chunk(j):
            loop(8, functools.partial(contract, j))
            hand_over(j)

            @pl.when(j > 0)
            def _():
                spread(j - 1)

        loop(NCH - 1, reduce_chunk)
        spread(NCH - 2)

        @pl.when(dom < 31)
        def _():
            to_upper().wait_send()

        @pl.when(dom > 0)
        def _():
            to_lower().wait_send()

    def relay(kind, t, j, b):
        piece(kind, t, j, b, kids[t][0], 0).wait_recv()
        for s in range(2):
            @pl.when(kids[t][s] >= 0)
            def _():
                piece(kind, t, j, b, kids[t][s], s).start()

    @pl.when(jnp.logical_not(root))
    def _():
        accs[...] = jnp.zeros_like(accs)
        acc[...] = jnp.zeros_like(acc)
        tmat_load.wait()
        mass_load.start()
        plan()
        pl.semaphore_wait(barrier, 20)

        def tick(k):
            for t in range(3):
                p = k - OFF * depths[t]
                count = FIRST[t + 1] - FIRST[t]

                @pl.when((p >= 0) & (p < T_HALO) & (p % PER < count))
                def _():
                    relay(0, t, p // PER, FIRST[t] + p % PER)

                h = HALO[t] + p - T_HALO

                @pl.when((p >= T_HALO) & (h < HALO[t + 1]))
                def _():
                    relay(1, t, h // 4, NB + h % 4)

                x = p - T_MASS

                @pl.when((x >= 0) & (p < T_END) & (x % PER < count))
                def _():
                    relay(2, t, x // PER, FIRST[t] + x % PER)

            m = k - (T_MASS + 4 * OFF)

            @pl.when(m == 0)
            def _():
                mass_load.wait()

            @pl.when((m >= 0) & (m < 18))
            def _():
                mass_step(1, 0, 8, m)

            @pl.when((m >= 12) & (m < 20))
            def _():
                contract(1, m - 12)

            @pl.when((m >= 18) & (m < 26))
            def _():
                i = m - 18
                for u in range(4):
                    turn(1, 0, 4 * i + u)
                contract(0, i)

            @pl.when((m >= 23) & (m < 31))
            def _():
                contract(2, m - 23)

            for j, at in ((1, 20), (0, 26), (2, 31)):
                @pl.when(m == at)
                def _():
                    hand_over(j)

            @pl.when((m == 24) | (m == 30))
            def _():
                spread((30 - m) // 6)

        loop(T_END + 4 * OFF, tick)

    last = NCH - 1
    loop(8, functools.partial(contract, last))
    hand_over(last)

    @pl.when(jnp.logical_not(root))
    def _():
        spread(last - 1)

    spread(last)

    for t in range(3):
        for s in range(2):
            @pl.when(kids[t][s] >= 0)
            def _():
                count = FIRST[t + 1] - FIRST[t]
                for kind, region in (
                    (0, ext.at[pl.ds(0, RAW), pl.ds(FIRST[t], count)]),
                    (1, ext.at[0, pl.ds(NB, HALO[t + 1] - HALO[t])]),
                    (2, xt.at[pl.ds(RAW, NCH - RAW), pl.ds(FIRST[t], count)]),
                ):
                    pltpu.make_async_remote_copy(
                        src_ref=region, dst_ref=region, send_sem=send_sem.at[t, s, kind],
                        recv_sem=raw_recv.at[0, 0], device_id={"col": kids[t][s]},
                    ).wait_send()
    def finish(j):
        @pl.when(core != j % 2)
        def _():
            pair_copy(j).wait_send()

        @pl.when(core == j % 2)
        def _():
            def sent(q):
                target, copy = part_copy(j, q)

                @pl.when(target != dom)
                def _():
                    copy.wait_send()

            loop(8, sent)

    loop(NCH, finish)

    def arrived(step):
        source = (chip + step + 1) % 16
        pltpu.make_async_remote_copy(
            src_ref=parts.at[0], dst_ref=parts.at[source],
            send_sem=part_send.at[0, 0], recv_sem=part_recv.at[source],
            device_id={"dom": source * 2 + core},
        ).wait_recv()

    loop(15, arrived)
    total = parts[0]
    for s in range(1, 16):
        total = total + parts[s]
    out_ref[...] = total


def couple(live, index, shared, tmat, mass):
    smem = pl.BlockSpec(memory_space=pltpu.SMEM)
    vmem = pl.BlockSpec(memory_space=pltpu.VMEM)
    anyspace = pl.BlockSpec(memory_space=pl.ANY)
    dma = pltpu.SemaphoreType.DMA
    return pl.pallas_call(
        couple_kernel,
        out_shape=jax.ShapeDtypeStruct((16, W), F32),
        in_specs=[smem, vmem, vmem, anyspace, anyspace],
        out_specs=vmem,
        scratch_shapes=[
            pltpu.VMEM((8, LIST), jnp.int32),
            pltpu.SMEM((8, LIST), jnp.int32),
            pltpu.VMEM((NCH, NB + 4, BS, MC), BF16),
            pltpu.VMEM((NCH, NB, MC, BS), BF16),
            pltpu.VMEM((NPAIR, BS, HALF), BF16),
            pltpu.VMEM((BS, HALF), F32),
            pltpu.VMEM((NB * BS, W), BF16),
            pltpu.VMEM((NS + 1, BS, BS), BF16),
            pltpu.VMEM((W, W), BF16),
            pltpu.VMEM((HALF, HALF), BF16),
            pltpu.VMEM((NCH, 4, BS, MC), BF16),
            pltpu.VMEM((NCH, MC, W), F32),
            pltpu.VMEM((2, MC, W), F32),
            pltpu.VMEM((16, 16, W), F32),
            dma((3,)), dma((2,)), dma((2,)), dma((RAW, NB + 4)), dma((NCH - RAW, NB)), dma((3, 2, 3)),
            dma((2,)), dma((2,)), dma((2, 8)), dma((16,)),
        ],
        compiler_params=pltpu.CompilerParams(
            collective_id=0, has_side_effects=True, vmem_limit_bytes=60 << 20
        ),
        name="couple",
    )(live, index, shared, tmat, mass)


def body(tmat, stored_mass_blocks, block_index, live_block_count, send_rows):
    return couple(live_block_count, block_index, send_rows, tmat, stored_mass_blocks)


def solution(mesh):
    return jax.shard_map(
        body,
        mesh=mesh,
        in_specs=(P("dom", "col"), P("dom", None, None), P("dom", None), P("dom"), P("dom", None)),
        out_specs=P("dom", "col"),
        check_vma=False,
    )
```

```python
import functools

import jax
import jax.numpy as jnp
from jax import lax
from jax.experimental import pallas as pl
from jax.experimental.pallas import tpu as pltpu
from jax.sharding import PartitionSpec as P

F32 = jnp.float32
BF16 = jnp.bfloat16
BS = 128
W = 512
NB = 32
NS = 256
NPAIR = (NS + NB) // 2
NCH = 4
MC = W // NCH
OFF = 5
PER = 11
RAW = 1
HALF = 256
LIST = 384

TREES = (
    ("00>10", "10>20", "20>21", "21>31", "10>11", "11>01", "20>30"),
    ("00>30", "30>20", "20>10", "30>31", "31>21", "21>11", "31>01"),
    ("00>01", "01>11", "11>21", "21>20", "01>31", "31>30", "11>10"),
)
FIRST = (0, 11, 22, 32)
HALO = (0, 2, 3, 4)
T_HALO = RAW * PER
T_MASS = T_HALO + 2
T_END = T_MASS + (NCH - RAW) * PER


def column_of(node):
    x, y = int(node[0]), int(node[1])
    return (x + 3) % 4 * 2 + 1 - y


def tree_tables():
    tables = []
    for edges in TREES:
        kids = [[-1, -1] for _ in range(8)]
        depth = [0] * 8
        for edge in edges:
            a, b = (column_of(n) for n in edge.split(">"))
            depth[b] = depth[a] + 1
            kids[a][0 if kids[a][0] < 0 else 1] = b
        tables.append((depth, [k[0] for k in kids], [k[1] for k in kids]))
    return tables


def pick(values, index):
    out = jnp.int32(values[0])
    for i, v in enumerate(values[1:], 1):
        out = jnp.where(index == i, jnp.int32(v), out)
    return out


def couple_kernel(
    live_ref, index_ref, shared_ref, tmat_hbm, mass_hbm, out_ref,
    order_v, order, ext, xt, steps, acc, tmat, mass, perm, eye, lists, accs, pairbuf, parts,
    load_sem, halo_send, halo_recv, raw_recv, x_recv, send_sem,
    pair_send, pair_recv, part_send, part_recv,
):
    col = lax.axis_index("col")
    dom = lax.axis_index("dom")
    core, zed, yhi = dom % 2, dom // 2 % 8, dom // 16
    chip = yhi * 8 + zed
    sibling = dom + 1 - 2 * core
    root = col == 7
    tables = tree_tables()
    depths = [pick(t[0], col) for t in tables]
    kids = [[pick(t[1], col), pick(t[2], col)] for t in tables]

    def loop(n, f):
        def step(i, _):
            f(i)
            return 0

        lax.fori_loop(0, n, step, 0)

    tmat_load = pltpu.make_async_copy(tmat_hbm, tmat, load_sem.at[0])
    tmat_load.start()
    mass_load = pltpu.make_async_copy(mass_hbm, mass.at[pl.ds(0, NS)], load_sem.at[1])

    barrier = pltpu.get_barrier_semaphore()
    xpos, ylo = col // 2, col % 2
    for near in ((xpos + 1) % 4 * 2 + ylo, (xpos + 3) % 4 * 2 + ylo, xpos * 2 + 1 - ylo):
        pl.semaphore_signal(barrier, inc=1, device_id={"col": near})
    for near in ((dom + 1) % 32, (dom + 31) % 32):
        pl.semaphore_signal(barrier, inc=1, device_id={"dom": near})

    def greet(step):
        far = (chip + step + 1) % 16
        pl.semaphore_signal(barrier, inc=1, device_id={"dom": far * 2 + core})

    loop(15, greet)

    mass[NS] = jnp.zeros((BS, BS), BF16)
    eye[...] = (
        lax.broadcasted_iota(jnp.int32, (HALF, HALF), 0) == lax.broadcasted_iota(jnp.int32, (HALF, HALF), 1)
    ).astype(BF16)

    def piece(kind, t, j, b, target, s):
        ref = ext.at[j, b] if kind < 2 else xt.at[RAW + j, b]
        sem = raw_recv.at[j, b] if kind < 2 else x_recv.at[j, b]
        return pltpu.make_async_remote_copy(
            src_ref=ref, dst_ref=ref, send_sem=send_sem.at[t, s, kind], recv_sem=sem,
            device_id={"col": target},
        )

    def plan():
        I32 = jnp.int32

        def iota(shape, axis):
            return lax.broadcasted_iota(I32, shape, axis)

        def add(condition, values, axis):
            return jnp.sum(jnp.where(condition, values, 0), axis=axis, keepdims=True)

        down = iota((NS, 1), 0)
        key = jnp.where(down < live_ref[0], index_ref[:, 0:1], NB)
        key_lane = add(iota((NS, NS), 0) == iota((NS, NS), 1), key, 0)
        before = add((key == key_lane) & (iota((NS, NS), 1) < iota((NS, NS), 0)), 1, 1)
        pairs_lane = (add(key == iota((NS, BS), 1), 1, 0) + 1) // 2
        pairs = (add(iota((NB, NS), 0) == key_lane, 1, 1) + 1) // 2
        base = add(iota((NS, BS), 1) < key, pairs_lane, 1)
        start = add(iota((NB, BS), 1) < iota((NB, BS), 0), pairs_lane, 1)
        place = jnp.where(key < NB, 2 * base + before, LIST)
        hit = place == iota((NS, LIST), 1)
        order_v[...] = jnp.zeros_like(order_v)
        order_v[0:1] = jnp.clip(NS - add(hit, NS - down, 0), 0, NS)
        order_v[1:2] = jnp.clip(add(hit, index_ref[:, 1:2], 0), 0, NB + 3)
        order_v[2:3] = 1 - add(start == iota((NB, LIST), 1), 1, 0)
        order_v[3:4] = jnp.clip(add(iota((NB, LIST), 0) <= iota((NB, LIST), 1), pairs, 0) - 1, 0, NPAIR - 1)
        copy = pltpu.make_async_copy(order_v, order, load_sem.at[2])
        copy.start()
        copy.wait()

    def mass_step(n, first, unr, k):
        prods = []
        for u in range(unr):
            q = k * unr + u
            blocks = jnp.concatenate([mass[order[0, 2 * q]], mass[order[0, 2 * q + 1]]], axis=1)
            rows = jnp.concatenate(
                [
                    jnp.concatenate([ext[first + v, order[1, 2 * q + w]] for v in range(n)], axis=1)
                    for w in range(2)
                ],
                axis=0,
            )
            prods.append(jnp.dot(blocks, rows, preferred_element_type=F32))
        total = acc[:, :n * MC]
        for u in range(unr):
            total = total * order[2, k * unr + u].astype(F32) + prods[u]
            steps[k * unr + u, :, :n * MC] = total.astype(BF16)
        acc[:, :n * MC] = total

    def turned_block(n, r):
        return lax.dot_general(
            eye[:n * MC, :n * MC], steps[order[3, r], :, :n * MC], (((1,), (1,)), ((), ())),
            preferred_element_type=F32,
        ).astype(BF16)

    def turn(n, first, r):
        done = turned_block(n, r)
        for v in range(n):
            xt[first + v, r] = done[v * MC:(v + 1) * MC]

    def contract(j, i):
        lhs = jnp.concatenate([xt[j, 4 * i + u] for u in range(4)], axis=1)
        rhs = tmat[pl.ds(pl.multiple_of(i * 512, 512), 512), :]
        accs[j] += jnp.dot(lhs, rhs, preferred_element_type=F32)

    def pair_copy(j):
        return pltpu.make_async_remote_copy(
            src_ref=accs.at[j], dst_ref=pairbuf.at[j // 2],
            send_sem=pair_send.at[j // 2], recv_sem=pair_recv.at[j // 2],
            device_id={"dom": sibling},
        )

    def part_copy(j, q):
        target = q // 4 * 16 + (q % 4 * 2 + j // 2) * 2 + core
        return target, pltpu.make_async_remote_copy(
            src_ref=accs.at[j, pl.ds(pl.multiple_of(q * 16, 16), 16)], dst_ref=parts.at[chip],
            send_sem=part_send.at[j // 2, q], recv_sem=part_recv.at[chip],
            device_id={"dom": target},
        )

    def hand_over(j):
        @pl.when(core != j % 2)
        def _():
            pair_copy(j).start()

    def spread(j):
        @pl.when(core == j % 2)
        def _():
            pair_copy(j).wait_recv()
            accs[j] += pairbuf[j // 2]

            def send_part(q):
                target, copy = part_copy(j, q)

                @pl.when(target != dom)
                def _():
                    copy.start()

                @pl.when(target == dom)
                def _():
                    parts[chip] = accs[j, pl.ds(pl.multiple_of(q * 16, 16), 16)]

            loop(8, send_part)

    def from_root(kind, t, j, b):
        piece(kind, t, j, b, pick(tables[t][1], jnp.int32(7)), 0).start()

    @pl.when(root)
    def _():
        mode = lax.broadcasted_iota(jnp.int32, (W, W), 0)
        place = lax.broadcasted_iota(jnp.int32, (W, W), 1)
        wanted = (place // 16 % 8) * 64 + (place // MC) * 16 + place % 16
        perm[...] = (mode == wanted).astype(BF16)
        plan()
        tmat_load.wait()
        mass_load.start()

        square = (2 * BS, 2 * BS)
        diagonal = lax.broadcasted_iota(jnp.int32, square, 0) == lax.broadcasted_iota(jnp.int32, square, 1)
        wanted_rows = [
            jnp.sum(jnp.where(diagonal, shared_ref[h:h + 1], 0), axis=1, keepdims=True) for h in range(2)
        ]
        idx = jnp.concatenate(wanted_rows, axis=0)
        accs[...] = jnp.zeros_like(accs)

        def gather(k):
            lane = lax.broadcasted_iota(jnp.int32, (4 * BS, 8 * BS), 1)
            picks = (idx == lane + k * 8 * BS).astype(BF16)
            rows = tmat[pl.ds(pl.multiple_of(k * 8 * BS, 8 * BS), 8 * BS), :]
            got = jnp.dot(picks, rows, preferred_element_type=F32)
            for h in range(4):
                accs[h] += got[h * BS:(h + 1) * BS]

        loop(NB // 8, gather)
        for h in range(4):
            got = jnp.dot(accs[h].astype(BF16), perm[...], preferred_element_type=F32).astype(BF16)
            for j in range(NCH):
                lists[j, h] = got[:, j * MC:(j + 1) * MC]

        pl.semaphore_wait(barrier, 20)
        def to_upper():
            return pltpu.make_async_remote_copy(
                src_ref=lists.at[:, pl.ds(2, 2)], dst_ref=ext.at[:, pl.ds(NB, 2)],
                send_sem=halo_send.at[0], recv_sem=halo_recv.at[0], device_id={"dom": (dom + 1) % 32},
            )

        def to_lower():
            return pltpu.make_async_remote_copy(
                src_ref=lists.at[:, pl.ds(0, 2)], dst_ref=ext.at[:, pl.ds(NB + 2, 2)],
                send_sem=halo_send.at[1], recv_sem=halo_recv.at[1], device_id={"dom": (dom + 31) % 32},
            )

        @pl.when(dom < 31)
        def _():
            to_upper().start()

        @pl.when(dom > 0)
        def _():
            to_lower().start()

        def trio(i, make, store):
            blocks = [FIRST[0] + i, FIRST[1] + i, jnp.minimum(FIRST[2] + i, NB - 1)]
            made = make(blocks)
            for t in range(3):
                @pl.when(i < FIRST[t + 1] - FIRST[t])
                def _():
                    store(t, blocks[t], made[t])

        def send_raw(i):
            def make(blocks):
                rows = jnp.concatenate([tmat[pl.ds(pl.multiple_of(b * BS, BS), BS), :] for b in blocks], axis=0)
                turned = jnp.dot(rows, perm[...], preferred_element_type=F32).astype(BF16)
                return [turned[t * BS:(t + 1) * BS] for t in range(3)]

            def store(t, b, turned):
                for j in range(NCH):
                    ext[j, b] = turned[:, j * MC:(j + 1) * MC]
                from_root(0, t, 0, b)

            trio(i, make, store)

        loop(PER, send_raw)
        mass_load.wait()

        @pl.when(dom > 0)
        def _():
            to_upper().wait_recv()

        @pl.when(dom == 0)
        def _():
            ext[:, NB:NB + 2] = jnp.zeros((NCH, 2, BS, MC), BF16)

        @pl.when(dom < 31)
        def _():
            to_lower().wait_recv()

        @pl.when(dom == 31)
        def _():
            ext[:, NB + 2:NB + 4] = jnp.zeros((NCH, 2, BS, MC), BF16)

        for t in range(3):
            for h in range(HALO[t], HALO[t + 1]):
                from_root(1, t, h // 4, NB + h % 4)

        def product(n, first, unr):
            acc[...] = jnp.zeros_like(acc)
            loop(NPAIR // unr, functools.partial(mass_step, n, first, unr))

        def send_mass(n, first, j, i):
            def store(t, b, done):
                for v in range(n):
                    xt[first + v, b] = done[v * MC:(v + 1) * MC]
                from_root(2, t, j, b)

            trio(i, lambda blocks: [turned_block(n, b) for b in blocks], store)

        def send_last(i):
            for t in range(3):
                @pl.when(i < FIRST[t + 1] - FIRST[t])
                def _():
                    from_root(2, t, 2, FIRST[t] + i)

        product(1, 1, 16)
        loop(PER, functools.partial(send_mass, 1, 1, 0))
        product(2, 2, 8)
        loop(PER, functools.partial(send_mass, 2, 2, 1))
        loop(PER, send_last)
        product(1, 0, 16)

        def turn_four(i):
            for u in range(4):
                turn(1, 0, 4 * i + u)

        loop(NB // 4, turn_four)
        accs[...] = jnp.zeros_like(accs)

        def reduce_chunk(j):
            loop(8, functools.partial(contract, j))
            hand_over(j)

            @pl.when(j > 0)
            def _():
                spread(j - 1)

        loop(NCH - 1, reduce_chunk)
        spread(NCH - 2)

        @pl.when(dom < 31)
        def _():
            to_upper().wait_send()

        @pl.when(dom > 0)
        def _():
            to_lower().wait_send()

    def relay(kind, t, j, b):
        piece(kind, t, j, b, kids[t][0], 0).wait_recv()
        for s in range(2):
            @pl.when(kids[t][s] >= 0)
            def _():
                piece(kind, t, j, b, kids[t][s], s).start()

    @pl.when(jnp.logical_not(root))
    def _():
        accs[...] = jnp.zeros_like(accs)
        acc[...] = jnp.zeros_like(acc)
        tmat_load.wait()
        mass_load.start()
        plan()
        pl.semaphore_wait(barrier, 20)

        def tick(k):
            for t in range(3):
                p = k - OFF * depths[t]
                count = FIRST[t + 1] - FIRST[t]

                @pl.when((p >= 0) & (p < T_HALO) & (p % PER < count))
                def _():
                    relay(0, t, p // PER, FIRST[t] + p % PER)

                h = HALO[t] + p - T_HALO

                @pl.when((p >= T_HALO) & (h < HALO[t + 1]))
                def _():
                    relay(1, t, h // 4, NB + h % 4)

                x = p - T_MASS

                @pl.when((x >= 0) & (p < T_END) & (x % PER < count))
                def _():
                    relay(2, t, x // PER, FIRST[t] + x % PER)

            m = k - (T_MASS + 4 * OFF)

            @pl.when(m == 0)
            def _():
                mass_load.wait()

            @pl.when((m >= 0) & (m < 18))
            def _():
                mass_step(1, 0, 8, m)

            @pl.when((m >= 12) & (m < 20))
            def _():
                contract(1, m - 12)

            @pl.when((m >= 18) & (m < 26))
            def _():
                i = m - 18
                for u in range(4):
                    turn(1, 0, 4 * i + u)
                contract(0, i)

            @pl.when((m >= 23) & (m < 31))
            def _():
                contract(2, m - 23)

            for j, at in ((1, 20), (0, 26), (2, 31)):
                @pl.when(m == at)
                def _():
                    hand_over(j)

            @pl.when((m == 24) | (m == 30))
            def _():
                spread((30 - m) // 6)

        loop(T_END + 4 * OFF, tick)

    last = NCH - 1
    loop(8, functools.partial(contract, last))
    hand_over(last)

    @pl.when(jnp.logical_not(root))
    def _():
        spread(last - 1)

    spread(last)

    for t in range(3):
        for s in range(2):
            @pl.when(kids[t][s] >= 0)
            def _():
                count = FIRST[t + 1] - FIRST[t]
                for kind, region in (
                    (0, ext.at[pl.ds(0, RAW), pl.ds(FIRST[t], count)]),
                    (1, ext.at[0, pl.ds(NB, HALO[t + 1] - HALO[t])]),
                    (2, xt.at[pl.ds(RAW, NCH - RAW), pl.ds(FIRST[t], count)]),
                ):
                    pltpu.make_async_remote_copy(
                        src_ref=region, dst_ref=region, send_sem=send_sem.at[t, s, kind],
                        recv_sem=raw_recv.at[0, 0], device_id={"col": kids[t][s]},
                    ).wait_send()
    def finish(j):
        @pl.when(core != j % 2)
        def _():
            pair_copy(j).wait_send()

        @pl.when(core == j % 2)
        def _():
            def sent(q):
                target, copy = part_copy(j, q)

                @pl.when(target != dom)
                def _():
                    copy.wait_send()

            loop(8, sent)

    loop(NCH, finish)

    def arrived(step):
        source = (chip + step + 1) % 16
        pltpu.make_async_remote_copy(
            src_ref=parts.at[0], dst_ref=parts.at[source],
            send_sem=part_send.at[0, 0], recv_sem=part_recv.at[source],
            device_id={"dom": source * 2 + core},
        ).wait_recv()

    loop(15, arrived)
    total = parts[0]
    for s in range(1, 16):
        total = total + parts[s]
    out_ref[...] = total


def couple(live, index, shared, tmat, mass):
    smem = pl.BlockSpec(memory_space=pltpu.SMEM)
    vmem = pl.BlockSpec(memory_space=pltpu.VMEM)
    anyspace = pl.BlockSpec(memory_space=pl.ANY)
    dma = pltpu.SemaphoreType.DMA
    return pl.pallas_call(
        couple_kernel,
        out_shape=jax.ShapeDtypeStruct((16, W), F32),
        in_specs=[smem, vmem, vmem, anyspace, anyspace],
        out_specs=vmem,
        scratch_shapes=[
            pltpu.VMEM((8, LIST), jnp.int32),
            pltpu.SMEM((8, LIST), jnp.int32),
            pltpu.VMEM((NCH, NB + 4, BS, MC), BF16),
            pltpu.VMEM((NCH, NB, MC, BS), BF16),
            pltpu.VMEM((NPAIR, BS, HALF), BF16),
            pltpu.VMEM((BS, HALF), F32),
            pltpu.VMEM((NB * BS, W), BF16),
            pltpu.VMEM((NS + 1, BS, BS), BF16),
            pltpu.VMEM((W, W), BF16),
            pltpu.VMEM((HALF, HALF), BF16),
            pltpu.VMEM((NCH, 4, BS, MC), BF16),
            pltpu.VMEM((NCH, MC, W), F32),
            pltpu.VMEM((2, MC, W), F32),
            pltpu.VMEM((16, 16, W), F32),
            dma((3,)), dma((2,)), dma((2,)), dma((RAW, NB + 4)), dma((NCH - RAW, NB)), dma((3, 2, 3)),
            dma((2,)), dma((2,)), dma((2, 8)), dma((16,)),
        ],
        compiler_params=pltpu.CompilerParams(
            collective_id=0, has_side_effects=True, vmem_limit_bytes=60 << 20
        ),
        name="couple",
    )(live, index, shared, tmat, mass)


def body(tmat, stored_mass_blocks, block_index, live_block_count, send_rows):
    return couple(live_block_count, block_index, send_rows, tmat, stored_mass_blocks)


def solution(mesh):
    return jax.shard_map(
        body,
        mesh=mesh,
        in_specs=(P("dom", "col"), P("dom", None, None), P("dom", None), P("dom"), P("dom", None)),
        out_specs=P("dom", "col"),
        check_vma=False,
    )
```

```python
import functools

import jax
import jax.numpy as jnp
from jax import lax
from jax.experimental import pallas as pl
from jax.experimental.pallas import tpu as pltpu
from jax.sharding import PartitionSpec as P

F32 = jnp.float32
BF16 = jnp.bfloat16
BS = 128
W = 512
NB = 32
NS = 256
NPAIR = (NS + NB) // 2
NCH = 4
MC = W // NCH
OFF = 5
PER = 11
RAW = 1
HALF = 256
LIST = 384

TREES = (
    ("00>10", "10>20", "20>21", "21>31", "10>11", "11>01", "20>30"),
    ("00>30", "30>20", "20>10", "30>31", "31>21", "21>11", "31>01"),
    ("00>01", "01>11", "11>21", "21>20", "01>31", "31>30", "11>10"),
)
FIRST = (0, 11, 22, 32)
HALO = (0, 2, 3, 4)
T_HALO = RAW * PER
T_MASS = T_HALO + 2
T_END = T_MASS + (NCH - RAW) * PER


def column_of(node):
    x, y = int(node[0]), int(node[1])
    return (x + 3) % 4 * 2 + 1 - y


def tree_tables():
    tables = []
    for edges in TREES:
        kids = [[-1, -1] for _ in range(8)]
        depth = [0] * 8
        for edge in edges:
            a, b = (column_of(n) for n in edge.split(">"))
            depth[b] = depth[a] + 1
            kids[a][0 if kids[a][0] < 0 else 1] = b
        tables.append((depth, [k[0] for k in kids], [k[1] for k in kids]))
    return tables


def pick(values, index):
    out = jnp.int32(values[0])
    for i, v in enumerate(values[1:], 1):
        out = jnp.where(index == i, jnp.int32(v), out)
    return out


def couple_kernel(
    live_ref, index_ref, shared_ref, tmat_hbm, mass_hbm, out_ref,
    order_v, order, ext, xt, steps, acc, tmat, mass, perm, eye, lists, accs, pairbuf, parts,
    load_sem, halo_send, halo_recv, raw_recv, x_recv, send_sem,
    pair_send, pair_recv, part_send, part_recv,
):
    col = lax.axis_index("col")
    dom = lax.axis_index("dom")
    core, zed, yhi = dom % 2, dom // 2 % 8, dom // 16
    chip = yhi * 8 + zed
    sibling = dom + 1 - 2 * core
    root = col == 7
    tables = tree_tables()
    depths = [pick(t[0], col) for t in tables]
    kids = [[pick(t[1], col), pick(t[2], col)] for t in tables]

    def loop(n, f):
        def step(i, _):
            f(i)
            return 0

        lax.fori_loop(0, n, step, 0)

    tmat_load = pltpu.make_async_copy(tmat_hbm, tmat, load_sem.at[0])
    tmat_load.start()
    mass_load = pltpu.make_async_copy(mass_hbm, mass.at[pl.ds(0, NS)], load_sem.at[1])

    barrier = pltpu.get_barrier_semaphore()
    xpos, ylo = col // 2, col % 2
    for near in ((xpos + 1) % 4 * 2 + ylo, (xpos + 3) % 4 * 2 + ylo, xpos * 2 + 1 - ylo):
        pl.semaphore_signal(barrier, inc=1, device_id={"col": near})
    for near in ((dom + 1) % 32, (dom + 31) % 32):
        pl.semaphore_signal(barrier, inc=1, device_id={"dom": near})

    def greet(step):
        far = (chip + step + 1) % 16
        pl.semaphore_signal(barrier, inc=1, device_id={"dom": far * 2 + core})

    loop(15, greet)

    mass[NS] = jnp.zeros((BS, BS), BF16)
    eye[...] = (
        lax.broadcasted_iota(jnp.int32, (HALF, HALF), 0) == lax.broadcasted_iota(jnp.int32, (HALF, HALF), 1)
    ).astype(BF16)

    def piece(kind, t, j, b, target, s):
        ref = ext.at[j, b] if kind < 2 else xt.at[RAW + j, b]
        sem = raw_recv.at[j, b] if kind < 2 else x_recv.at[j, b]
        return pltpu.make_async_remote_copy(
            src_ref=ref, dst_ref=ref, send_sem=send_sem.at[t, s, kind], recv_sem=sem,
            device_id={"col": target},
        )

    def plan():
        I32 = jnp.int32

        def iota(shape, axis):
            return lax.broadcasted_iota(I32, shape, axis)

        def add(condition, values, axis):
            return jnp.sum(jnp.where(condition, values, 0), axis=axis, keepdims=True)

        down = iota((NS, 1), 0)
        key = jnp.where(down < live_ref[0], index_ref[:, 0:1], NB)
        key_lane = add(iota((NS, NS), 0) == iota((NS, NS), 1), key, 0)
        before = add((key == key_lane) & (iota((NS, NS), 1) < iota((NS, NS), 0)), 1, 1)
        pairs_lane = (add(key == iota((NS, BS), 1), 1, 0) + 1) // 2
        pairs = (add(iota((NB, NS), 0) == key_lane, 1, 1) + 1) // 2
        base = add(iota((NS, BS), 1) < key, pairs_lane, 1)
        start = add(iota((NB, BS), 1) < iota((NB, BS), 0), pairs_lane, 1)
        place = jnp.where(key < NB, 2 * base + before, LIST)
        hit = place == iota((NS, LIST), 1)
        order_v[...] = jnp.zeros_like(order_v)
        order_v[0:1] = jnp.clip(NS - add(hit, NS - down, 0), 0, NS)
        order_v[1:2] = jnp.clip(add(hit, index_ref[:, 1:2], 0), 0, NB + 3)
        order_v[2:3] = 1 - add(start == iota((NB, LIST), 1), 1, 0)
        order_v[3:4] = jnp.clip(add(iota((NB, LIST), 0) <= iota((NB, LIST), 1), pairs, 0) - 1, 0, NPAIR - 1)
        copy = pltpu.make_async_copy(order_v, order, load_sem.at[2])
        copy.start()
        copy.wait()

    def mass_step(n, first, unr, k):
        prods = []
        for u in range(unr):
            q = k * unr + u
            blocks = jnp.concatenate([mass[order[0, 2 * q]], mass[order[0, 2 * q + 1]]], axis=1)
            rows = jnp.concatenate(
                [
                    jnp.concatenate([ext[first + v, order[1, 2 * q + w]] for v in range(n)], axis=1)
                    for w in range(2)
                ],
                axis=0,
            )
            prods.append(jnp.dot(blocks, rows, preferred_element_type=F32))
        total = acc[:, :n * MC]
        for u in range(unr):
            total = total * order[2, k * unr + u].astype(F32) + prods[u]
            steps[k * unr + u, :, :n * MC] = total.astype(BF16)
        acc[:, :n * MC] = total

    def turned_block(n, r):
        return lax.dot_general(
            eye[:n * MC, :n * MC], steps[order[3, r], :, :n * MC], (((1,), (1,)), ((), ())),
            preferred_element_type=F32,
        ).astype(BF16)

    def turn(n, first, r):
        done = turned_block(n, r)
        for v in range(n):
            xt[first + v, r] = done[v * MC:(v + 1) * MC]

    def contract(j, i):
        lhs = jnp.concatenate([xt[j, 4 * i + u] for u in range(4)], axis=1)
        rhs = tmat[pl.ds(pl.multiple_of(i * 512, 512), 512), :]
        accs[j] += jnp.dot(lhs, rhs, preferred_element_type=F32)

    def pair_copy(j):
        return pltpu.make_async_remote_copy(
            src_ref=accs.at[j], dst_ref=pairbuf.at[j // 2],
            send_sem=pair_send.at[j // 2], recv_sem=pair_recv.at[j // 2],
            device_id={"dom": sibling},
        )

    def part_copy(j, q):
        target = q // 4 * 16 + (q % 4 * 2 + j // 2) * 2 + core
        return target, pltpu.make_async_remote_copy(
            src_ref=accs.at[j, pl.ds(pl.multiple_of(q * 16, 16), 16)], dst_ref=parts.at[chip],
            send_sem=part_send.at[j // 2, q], recv_sem=part_recv.at[chip],
            device_id={"dom": target},
        )

    def hand_over(j):
        @pl.when(core != j % 2)
        def _():
            pair_copy(j).start()

    def spread(j):
        @pl.when(core == j % 2)
        def _():
            pair_copy(j).wait_recv()
            accs[j] += pairbuf[j // 2]

            def send_part(q):
                target, copy = part_copy(j, q)

                @pl.when(target != dom)
                def _():
                    copy.start()

                @pl.when(target == dom)
                def _():
                    parts[chip] = accs[j, pl.ds(pl.multiple_of(q * 16, 16), 16)]

            loop(8, send_part)

    def from_root(kind, t, j, b):
        piece(kind, t, j, b, pick(tables[t][1], jnp.int32(7)), 0).start()

    @pl.when(root)
    def _():
        mode = lax.broadcasted_iota(jnp.int32, (W, W), 0)
        place = lax.broadcasted_iota(jnp.int32, (W, W), 1)
        wanted = (place // 16 % 8) * 64 + (place // MC) * 16 + place % 16
        perm[...] = (mode == wanted).astype(BF16)
        plan()
        tmat_load.wait()
        mass_load.start()

        square = (2 * BS, 2 * BS)
        diagonal = lax.broadcasted_iota(jnp.int32, square, 0) == lax.broadcasted_iota(jnp.int32, square, 1)
        wanted_rows = [
            jnp.sum(jnp.where(diagonal, shared_ref[h:h + 1], 0), axis=1, keepdims=True) for h in range(2)
        ]
        idx = jnp.concatenate(wanted_rows, axis=0)
        accs[...] = jnp.zeros_like(accs)

        def gather(k):
            lane = lax.broadcasted_iota(jnp.int32, (4 * BS, 8 * BS), 1)
            picks = (idx == lane + k * 8 * BS).astype(BF16)
            rows = tmat[pl.ds(pl.multiple_of(k * 8 * BS, 8 * BS), 8 * BS), :]
            got = jnp.dot(picks, rows, preferred_element_type=F32)
            for h in range(4):
                accs[h] += got[h * BS:(h + 1) * BS]

        loop(NB // 8, gather)
        got = jnp.concatenate([accs[h].astype(BF16) for h in range(4)], axis=0)
        got = jnp.dot(got, perm[...], preferred_element_type=F32).astype(BF16)
        for h in range(4):
            for j in range(NCH):
                lists[j, h] = got[h * BS:(h + 1) * BS, j * MC:(j + 1) * MC]

        pl.semaphore_wait(barrier, 20)
        def to_upper():
            return pltpu.make_async_remote_copy(
                src_ref=lists.at[:, pl.ds(2, 2)], dst_ref=ext.at[:, pl.ds(NB, 2)],
                send_sem=halo_send.at[0], recv_sem=halo_recv.at[0], device_id={"dom": (dom + 1) % 32},
            )

        def to_lower():
            return pltpu.make_async_remote_copy(
                src_ref=lists.at[:, pl.ds(0, 2)], dst_ref=ext.at[:, pl.ds(NB + 2, 2)],
                send_sem=halo_send.at[1], recv_sem=halo_recv.at[1], device_id={"dom": (dom + 31) % 32},
            )

        @pl.when(dom < 31)
        def _():
            to_upper().start()

        @pl.when(dom > 0)
        def _():
            to_lower().start()

        def trio(i, make, store):
            blocks = [FIRST[0] + i, FIRST[1] + i, jnp.minimum(FIRST[2] + i, NB - 1)]
            made = make(blocks)
            for t in range(3):
                @pl.when(i < FIRST[t + 1] - FIRST[t])
                def _():
                    store(t, blocks[t], made[t])

        def send_raw(i):
            def make(blocks):
                rows = jnp.concatenate([tmat[pl.ds(pl.multiple_of(b * BS, BS), BS), :] for b in blocks], axis=0)
                turned = jnp.dot(rows, perm[...], preferred_element_type=F32).astype(BF16)
                return [turned[t * BS:(t + 1) * BS] for t in range(3)]

            def store(t, b, turned):
                for j in range(NCH):
                    ext[j, b] = turned[:, j * MC:(j + 1) * MC]
                from_root(0, t, 0, b)

            trio(i, make, store)

        loop(PER, send_raw)
        mass_load.wait()

        @pl.when(dom > 0)
        def _():
            to_upper().wait_recv()

        @pl.when(dom == 0)
        def _():
            ext[:, NB:NB + 2] = jnp.zeros((NCH, 2, BS, MC), BF16)

        @pl.when(dom < 31)
        def _():
            to_lower().wait_recv()

        @pl.when(dom == 31)
        def _():
            ext[:, NB + 2:NB + 4] = jnp.zeros((NCH, 2, BS, MC), BF16)

        for t in range(3):
            for h in range(HALO[t], HALO[t + 1]):
                from_root(1, t, h // 4, NB + h % 4)

        def product(n, first, unr):
            acc[...] = jnp.zeros_like(acc)
            loop(NPAIR // unr, functools.partial(mass_step, n, first, unr))

        def send_mass(n, first, j, i):
            def store(t, b, done):
                for v in range(n):
                    xt[first + v, b] = done[v * MC:(v + 1) * MC]
                from_root(2, t, j, b)

            trio(i, lambda blocks: [turned_block(n, b) for b in blocks], store)

        def send_last(i):
            for t in range(3):
                @pl.when(i < FIRST[t + 1] - FIRST[t])
                def _():
                    from_root(2, t, 2, FIRST[t] + i)

        product(1, 1, 24)
        loop(PER, functools.partial(send_mass, 1, 1, 0))
        product(2, 2, 12)
        loop(PER, functools.partial(send_mass, 2, 2, 1))
        loop(PER, send_last)
        product(1, 0, 16)

        def turn_four(i):
            for u in range(4):
                turn(1, 0, 4 * i + u)

        loop(NB // 4, turn_four)
        accs[...] = jnp.zeros_like(accs)

        def reduce_chunk(j):
            loop(8, functools.partial(contract, j))
            hand_over(j)

            @pl.when(j > 0)
            def _():
                spread(j - 1)

        loop(NCH - 1, reduce_chunk)
        spread(NCH - 2)

        @pl.when(dom < 31)
        def _():
            to_upper().wait_send()

        @pl.when(dom > 0)
        def _():
            to_lower().wait_send()

    def relay(kind, t, j, b):
        piece(kind, t, j, b, kids[t][0], 0).wait_recv()
        for s in range(2):
            @pl.when(kids[t][s] >= 0)
            def _():
                piece(kind, t, j, b, kids[t][s], s).start()

    @pl.when(jnp.logical_not(root))
    def _():
        accs[...] = jnp.zeros_like(accs)
        acc[...] = jnp.zeros_like(acc)
        tmat_load.wait()
        mass_load.start()
        plan()
        pl.semaphore_wait(barrier, 20)

        def tick(k):
            for t in range(3):
                p = k - OFF * depths[t]
                count = FIRST[t + 1] - FIRST[t]

                @pl.when((p >= 0) & (p < T_HALO) & (p % PER < count))
                def _():
                    relay(0, t, p // PER, FIRST[t] + p % PER)

                h = HALO[t] + p - T_HALO

                @pl.when((p >= T_HALO) & (h < HALO[t + 1]))
                def _():
                    relay(1, t, h // 4, NB + h % 4)

                x = p - T_MASS

                @pl.when((x >= 0) & (p < T_END) & (x % PER < count))
                def _():
                    relay(2, t, x // PER, FIRST[t] + x % PER)

            m = k - (T_MASS + 4 * OFF)

            @pl.when(m == 0)
            def _():
                mass_load.wait()

            @pl.when((m >= 0) & (m < 18))
            def _():
                mass_step(1, 0, 8, m)

            @pl.when((m >= 12) & (m < 20))
            def _():
                contract(1, m - 12)

            @pl.when((m >= 18) & (m < 26))
            def _():
                i = m - 18
                for u in range(4):
                    turn(1, 0, 4 * i + u)
                contract(0, i)

            @pl.when((m >= 23) & (m < 31))
            def _():
                contract(2, m - 23)

            for j, at in ((1, 20), (0, 26), (2, 31)):
                @pl.when(m == at)
                def _():
                    hand_over(j)

            @pl.when((m == 24) | (m == 30))
            def _():
                spread((30 - m) // 6)

        loop(T_END + 4 * OFF, tick)

    last = NCH - 1
    loop(8, functools.partial(contract, last))
    hand_over(last)

    @pl.when(jnp.logical_not(root))
    def _():
        spread(last - 1)

    spread(last)

    for t in range(3):
        for s in range(2):
            @pl.when(kids[t][s] >= 0)
            def _():
                count = FIRST[t + 1] - FIRST[t]
                for kind, region in (
                    (0, ext.at[pl.ds(0, RAW), pl.ds(FIRST[t], count)]),
                    (1, ext.at[0, pl.ds(NB, HALO[t + 1] - HALO[t])]),
                    (2, xt.at[pl.ds(RAW, NCH - RAW), pl.ds(FIRST[t], count)]),
                ):
                    pltpu.make_async_remote_copy(
                        src_ref=region, dst_ref=region, send_sem=send_sem.at[t, s, kind],
                        recv_sem=raw_recv.at[0, 0], device_id={"col": kids[t][s]},
                    ).wait_send()
    def finish(j):
        @pl.when(core != j % 2)
        def _():
            pair_copy(j).wait_send()

        @pl.when(core == j % 2)
        def _():
            def sent(q):
                target, copy = part_copy(j, q)

                @pl.when(target != dom)
                def _():
                    copy.wait_send()

            loop(8, sent)

    loop(NCH, finish)

    def arrived(step):
        source = (chip + step + 1) % 16
        pltpu.make_async_remote_copy(
            src_ref=parts.at[0], dst_ref=parts.at[source],
            send_sem=part_send.at[0, 0], recv_sem=part_recv.at[source],
            device_id={"dom": source * 2 + core},
        ).wait_recv()

    loop(15, arrived)
    total = parts[0]
    for s in range(1, 16):
        total = total + parts[s]
    out_ref[...] = total


def couple(live, index, shared, tmat, mass):
    smem = pl.BlockSpec(memory_space=pltpu.SMEM)
    vmem = pl.BlockSpec(memory_space=pltpu.VMEM)
    anyspace = pl.BlockSpec(memory_space=pl.ANY)
    dma = pltpu.SemaphoreType.DMA
    return pl.pallas_call(
        couple_kernel,
        out_shape=jax.ShapeDtypeStruct((16, W), F32),
        in_specs=[smem, vmem, vmem, anyspace, anyspace],
        out_specs=vmem,
        scratch_shapes=[
            pltpu.VMEM((8, LIST), jnp.int32),
            pltpu.SMEM((8, LIST), jnp.int32),
            pltpu.VMEM((NCH, NB + 4, BS, MC), BF16),
            pltpu.VMEM((NCH, NB, MC, BS), BF16),
            pltpu.VMEM((NPAIR, BS, HALF), BF16),
            pltpu.VMEM((BS, HALF), F32),
            pltpu.VMEM((NB * BS, W), BF16),
            pltpu.VMEM((NS + 1, BS, BS), BF16),
            pltpu.VMEM((W, W), BF16),
            pltpu.VMEM((HALF, HALF), BF16),
            pltpu.VMEM((NCH, 4, BS, MC), BF16),
            pltpu.VMEM((NCH, MC, W), F32),
            pltpu.VMEM((2, MC, W), F32),
            pltpu.VMEM((16, 16, W), F32),
            dma((3,)), dma((2,)), dma((2,)), dma((RAW, NB + 4)), dma((NCH - RAW, NB)), dma((3, 2, 3)),
            dma((2,)), dma((2,)), dma((2, 8)), dma((16,)),
        ],
        compiler_params=pltpu.CompilerParams(
            collective_id=0, has_side_effects=True, vmem_limit_bytes=60 << 20
        ),
        name="couple",
    )(live, index, shared, tmat, mass)


def body(tmat, stored_mass_blocks, block_index, live_block_count, send_rows):
    return couple(live_block_count, block_index, send_rows, tmat, stored_mass_blocks)


def solution(mesh):
    return jax.shard_map(
        body,
        mesh=mesh,
        in_specs=(P("dom", "col"), P("dom", None, None), P("dom", None), P("dom"), P("dom", None)),
        out_specs=P("dom", "col"),
        check_vma=False,
    )
```

```python
import functools

import jax
import jax.numpy as jnp
from jax import lax
from jax.experimental import pallas as pl
from jax.experimental.pallas import tpu as pltpu
from jax.sharding import PartitionSpec as P

F32 = jnp.float32
BF16 = jnp.bfloat16
BS = 128
W = 512
NB = 32
NS = 256
NPAIR = (NS + NB) // 2
NCH = 4
MC = W // NCH
OFF = 5
PER = 11
RAW = 1
HALF = 256
LIST = 384

TREES = (
    ("00>10", "10>20", "20>21", "21>31", "10>11", "11>01", "20>30"),
    ("00>30", "30>20", "20>10", "30>31", "31>21", "21>11", "31>01"),
    ("00>01", "01>11", "11>21", "21>20", "01>31", "31>30", "11>10"),
)
FIRST = (0, 11, 22, 32)
HALO = (0, 2, 3, 4)
T_HALO = RAW * PER
T_MASS = T_HALO + 2
T_END = T_MASS + (NCH - RAW) * PER


def column_of(node):
    x, y = int(node[0]), int(node[1])
    return (x + 3) % 4 * 2 + 1 - y


def tree_tables():
    tables = []
    for edges in TREES:
        kids = [[-1, -1] for _ in range(8)]
        depth = [0] * 8
        for edge in edges:
            a, b = (column_of(n) for n in edge.split(">"))
            depth[b] = depth[a] + 1
            kids[a][0 if kids[a][0] < 0 else 1] = b
        tables.append((depth, [k[0] for k in kids], [k[1] for k in kids]))
    return tables


def pick(values, index):
    out = jnp.int32(values[0])
    for i, v in enumerate(values[1:], 1):
        out = jnp.where(index == i, jnp.int32(v), out)
    return out


def couple_kernel(
    live_ref, index_ref, shared_ref, tmat_hbm, mass_hbm, out_ref,
    order_v, order, ext, xt, steps, acc, tmat, mass, perm, eye, lists, accs, pairbuf, parts,
    load_sem, halo_send, halo_recv, raw_recv, x_recv, send_sem,
    pair_send, pair_recv, part_send, part_recv,
):
    col = lax.axis_index("col")
    dom = lax.axis_index("dom")
    core, zed, yhi = dom % 2, dom // 2 % 8, dom // 16
    chip = yhi * 8 + zed
    sibling = dom + 1 - 2 * core
    root = col == 7
    tables = tree_tables()
    depths = [pick(t[0], col) for t in tables]
    kids = [[pick(t[1], col), pick(t[2], col)] for t in tables]

    def loop(n, f):
        def step(i, _):
            f(i)
            return 0

        lax.fori_loop(0, n, step, 0)

    tmat_load = pltpu.make_async_copy(tmat_hbm, tmat, load_sem.at[0])
    tmat_load.start()
    mass_load = pltpu.make_async_copy(mass_hbm, mass.at[pl.ds(0, NS)], load_sem.at[1])

    barrier = pltpu.get_barrier_semaphore()
    xpos, ylo = col // 2, col % 2
    for near in ((xpos + 1) % 4 * 2 + ylo, (xpos + 3) % 4 * 2 + ylo, xpos * 2 + 1 - ylo):
        pl.semaphore_signal(barrier, inc=1, device_id={"col": near})
    for near in ((dom + 1) % 32, (dom + 31) % 32):
        pl.semaphore_signal(barrier, inc=1, device_id={"dom": near})

    def greet(step):
        far = (chip + step + 1) % 16
        pl.semaphore_signal(barrier, inc=1, device_id={"dom": far * 2 + core})

    loop(15, greet)

    mass[NS] = jnp.zeros((BS, BS), BF16)
    eye[...] = (
        lax.broadcasted_iota(jnp.int32, (HALF, HALF), 0) == lax.broadcasted_iota(jnp.int32, (HALF, HALF), 1)
    ).astype(BF16)

    def piece(kind, t, j, b, target, s):
        ref = ext.at[j, b] if kind < 2 else xt.at[RAW + j, b]
        sem = raw_recv.at[j, b] if kind < 2 else x_recv.at[j, b]
        return pltpu.make_async_remote_copy(
            src_ref=ref, dst_ref=ref, send_sem=send_sem.at[t, s, kind], recv_sem=sem,
            device_id={"col": target},
        )

    def plan():
        I32 = jnp.int32

        def iota(shape, axis):
            return lax.broadcasted_iota(I32, shape, axis)

        def add(condition, values, axis):
            return jnp.sum(jnp.where(condition, values, 0), axis=axis, keepdims=True)

        down = iota((NS, 1), 0)
        key = jnp.where(down < live_ref[0], index_ref[:, 0:1], NB)
        key_lane = add(iota((NS, NS), 0) == iota((NS, NS), 1), key, 0)
        before = add((key == key_lane) & (iota((NS, NS), 1) < iota((NS, NS), 0)), 1, 1)
        pairs_lane = (add(key == iota((NS, BS), 1), 1, 0) + 1) // 2
        pairs = (add(iota((NB, NS), 0) == key_lane, 1, 1) + 1) // 2
        base = add(iota((NS, BS), 1) < key, pairs_lane, 1)
        start = add(iota((NB, BS), 1) < iota((NB, BS), 0), pairs_lane, 1)
        place = jnp.where(key < NB, 2 * base + before, LIST)
        hit = place == iota((NS, LIST), 1)
        order_v[...] = jnp.zeros_like(order_v)
        order_v[0:1] = jnp.clip(NS - add(hit, NS - down, 0), 0, NS)
        order_v[1:2] = jnp.clip(add(hit, index_ref[:, 1:2], 0), 0, NB + 3)
        order_v[2:3] = 1 - add(start == iota((NB, LIST), 1), 1, 0)
        order_v[3:4] = jnp.clip(add(iota((NB, LIST), 0) <= iota((NB, LIST), 1), pairs, 0) - 1, 0, NPAIR - 1)
        copy = pltpu.make_async_copy(order_v, order, load_sem.at[2])
        copy.start()
        copy.wait()

    def mass_step(n, first, unr, k):
        prods = []
        for u in range(unr):
            q = k * unr + u
            blocks = jnp.concatenate([mass[order[0, 2 * q]], mass[order[0, 2 * q + 1]]], axis=1)
            rows = jnp.concatenate(
                [
                    jnp.concatenate([ext[first + v, order[1, 2 * q + w]] for v in range(n)], axis=1)
                    for w in range(2)
                ],
                axis=0,
            )
            prods.append(jnp.dot(blocks, rows, preferred_element_type=F32))
        total = acc[:, :n * MC]
        for u in range(unr):
            total = total * order[2, k * unr + u].astype(F32) + prods[u]
            steps[k * unr + u, :, :n * MC] = total.astype(BF16)
        acc[:, :n * MC] = total

    def turned_block(n, r):
        return lax.dot_general(
            eye[:n * MC, :n * MC], steps[order[3, r], :, :n * MC], (((1,), (1,)), ((), ())),
            preferred_element_type=F32,
        ).astype(BF16)

    def turn(n, first, r):
        done = turned_block(n, r)
        for v in range(n):
            xt[first + v, r] = done[v * MC:(v + 1) * MC]

    def contract(j, i):
        lhs = jnp.concatenate([xt[j, 4 * i + u] for u in range(4)], axis=1)
        rhs = tmat[pl.ds(pl.multiple_of(i * 512, 512), 512), :]
        accs[j] += jnp.dot(lhs, rhs, preferred_element_type=F32)

    def pair_copy(j):
        return pltpu.make_async_remote_copy(
            src_ref=accs.at[j], dst_ref=pairbuf.at[j // 2],
            send_sem=pair_send.at[j // 2], recv_sem=pair_recv.at[j // 2],
            device_id={"dom": sibling},
        )

    def part_copy(j, q):
        target = q // 4 * 16 + (q % 4 * 2 + j // 2) * 2 + core
        return target, pltpu.make_async_remote_copy(
            src_ref=accs.at[j, pl.ds(pl.multiple_of(q * 16, 16), 16)], dst_ref=parts.at[chip],
            send_sem=part_send.at[j // 2, q], recv_sem=part_recv.at[chip],
            device_id={"dom": target},
        )

    def hand_over(j):
        @pl.when(core != j % 2)
        def _():
            pair_copy(j).start()

    def spread(j):
        @pl.when(core == j % 2)
        def _():
            pair_copy(j).wait_recv()
            accs[j] += pairbuf[j // 2]

            def send_part(q):
                target, copy = part_copy(j, q)

                @pl.when(target != dom)
                def _():
                    copy.start()

                @pl.when(target == dom)
                def _():
                    parts[chip] = accs[j, pl.ds(pl.multiple_of(q * 16, 16), 16)]

            loop(8, send_part)

    def from_root(kind, t, j, b):
        piece(kind, t, j, b, pick(tables[t][1], jnp.int32(7)), 0).start()

    @pl.when(root)
    def _():
        mode = lax.broadcasted_iota(jnp.int32, (W, W), 0)
        place = lax.broadcasted_iota(jnp.int32, (W, W), 1)
        wanted = (place // 16 % 8) * 64 + (place // MC) * 16 + place % 16
        perm[...] = (mode == wanted).astype(BF16)
        plan()
        tmat_load.wait()
        mass_load.start()

        square = (2 * BS, 2 * BS)
        diagonal = lax.broadcasted_iota(jnp.int32, square, 0) == lax.broadcasted_iota(jnp.int32, square, 1)
        wanted_rows = [
            jnp.sum(jnp.where(diagonal, shared_ref[h:h + 1], 0), axis=1, keepdims=True) for h in range(2)
        ]
        idx = jnp.concatenate(wanted_rows, axis=0)
        accs[...] = jnp.zeros_like(accs)

        def gather(k):
            lane = lax.broadcasted_iota(jnp.int32, (4 * BS, 8 * BS), 1)
            picks = (idx == lane + k * 8 * BS).astype(BF16)
            rows = tmat[pl.ds(pl.multiple_of(k * 8 * BS, 8 * BS), 8 * BS), :]
            got = jnp.dot(picks, rows, preferred_element_type=F32)
            for h in range(4):
                accs[h] += got[h * BS:(h + 1) * BS]

        loop(NB // 8, gather)
        got = jnp.concatenate([accs[h].astype(BF16) for h in range(4)], axis=0)
        got = jnp.dot(got, perm[...], preferred_element_type=F32).astype(BF16)
        for h in range(4):
            for j in range(NCH):
                lists[j, h] = got[h * BS:(h + 1) * BS, j * MC:(j + 1) * MC]

        pl.semaphore_wait(barrier, 20)
        def to_upper():
            return pltpu.make_async_remote_copy(
                src_ref=lists.at[:, pl.ds(2, 2)], dst_ref=ext.at[:, pl.ds(NB, 2)],
                send_sem=halo_send.at[0], recv_sem=halo_recv.at[0], device_id={"dom": (dom + 1) % 32},
            )

        def to_lower():
            return pltpu.make_async_remote_copy(
                src_ref=lists.at[:, pl.ds(0, 2)], dst_ref=ext.at[:, pl.ds(NB + 2, 2)],
                send_sem=halo_send.at[1], recv_sem=halo_recv.at[1], device_id={"dom": (dom + 31) % 32},
            )

        @pl.when(dom < 31)
        def _():
            to_upper().start()

        @pl.when(dom > 0)
        def _():
            to_lower().start()

        def trio(i, make, store):
            blocks = [FIRST[0] + i, FIRST[1] + i, jnp.minimum(FIRST[2] + i, NB - 1)]
            made = make(blocks)
            for t in range(3):
                @pl.when(i < FIRST[t + 1] - FIRST[t])
                def _():
                    store(t, blocks[t], made[t])

        def send_raw(i):
            def make(blocks):
                rows = jnp.concatenate([tmat[pl.ds(pl.multiple_of(b * BS, BS), BS), :] for b in blocks], axis=0)
                turned = jnp.dot(rows, perm[...], preferred_element_type=F32).astype(BF16)
                return [turned[t * BS:(t + 1) * BS] for t in range(3)]

            def store(t, b, turned):
                for j in range(NCH):
                    ext[j, b] = turned[:, j * MC:(j + 1) * MC]
                from_root(0, t, 0, b)

            trio(i, make, store)

        loop(PER, send_raw)
        mass_load.wait()

        @pl.when(dom > 0)
        def _():
            to_upper().wait_recv()

        @pl.when(dom == 0)
        def _():
            ext[:, NB:NB + 2] = jnp.zeros((NCH, 2, BS, MC), BF16)

        @pl.when(dom < 31)
        def _():
            to_lower().wait_recv()

        @pl.when(dom == 31)
        def _():
            ext[:, NB + 2:NB + 4] = jnp.zeros((NCH, 2, BS, MC), BF16)

        for t in range(3):
            for h in range(HALO[t], HALO[t + 1]):
                from_root(1, t, h // 4, NB + h % 4)

        def product(n, first, unr):
            acc[...] = jnp.zeros_like(acc)
            loop(NPAIR // unr, functools.partial(mass_step, n, first, unr))

        def send_mass(n, first, j, i):
            def store(t, b, done):
                for v in range(n):
                    xt[first + v, b] = done[v * MC:(v + 1) * MC]
                from_root(2, t, j, b)

            trio(i, lambda blocks: [turned_block(n, b) for b in blocks], store)

        def send_last(i):
            for t in range(3):
                @pl.when(i < FIRST[t + 1] - FIRST[t])
                def _():
                    from_root(2, t, 2, FIRST[t] + i)

        product(1, 1, 24)
        loop(PER, functools.partial(send_mass, 1, 1, 0))
        product(2, 2, 12)
        loop(PER, functools.partial(send_mass, 2, 2, 1))
        loop(PER, send_last)
        product(1, 0, 16)

        def turn_four(i):
            for u in range(4):
                turn(1, 0, 4 * i + u)

        loop(NB // 4, turn_four)
        accs[...] = jnp.zeros_like(accs)

        def reduce_chunk(j):
            loop(8, functools.partial(contract, j))
            hand_over(j)

            @pl.when(j > 0)
            def _():
                spread(j - 1)

        loop(NCH - 1, reduce_chunk)
        spread(NCH - 2)

        @pl.when(dom < 31)
        def _():
            to_upper().wait_send()

        @pl.when(dom > 0)
        def _():
            to_lower().wait_send()

    def relay(kind, t, j, b):
        piece(kind, t, j, b, kids[t][0], 0).wait_recv()
        for s in range(2):
            @pl.when(kids[t][s] >= 0)
            def _():
                piece(kind, t, j, b, kids[t][s], s).start()

    @pl.when(jnp.logical_not(root))
    def _():
        accs[...] = jnp.zeros_like(accs)
        acc[...] = jnp.zeros_like(acc)
        tmat_load.wait()
        mass_load.start()
        plan()
        pl.semaphore_wait(barrier, 20)

        def tick(k):
            for t in range(3):
                p = k - OFF * depths[t]
                count = FIRST[t + 1] - FIRST[t]

                @pl.when((p >= 0) & (p < T_HALO) & (p % PER < count))
                def _():
                    relay(0, t, p // PER, FIRST[t] + p % PER)

                h = HALO[t] + p - T_HALO

                @pl.when((p >= T_HALO) & (h < HALO[t + 1]))
                def _():
                    relay(1, t, h // 4, NB + h % 4)

                x = p - T_MASS

                @pl.when((x >= 0) & (p < T_END) & (x % PER < count))
                def _():
                    relay(2, t, x // PER, FIRST[t] + x % PER)

            m = k - (T_MASS + 4 * OFF)

            @pl.when(m == 0)
            def _():
                mass_load.wait()

            @pl.when((m >= 0) & (m < 18))
            def _():
                mass_step(1, 0, 8, m)

            @pl.when((m >= 12) & (m < 20))
            def _():
                contract(1, m - 12)

            @pl.when((m >= 18) & (m < 26))
            def _():
                i = m - 18
                for u in range(4):
                    turn(1, 0, 4 * i + u)
                contract(0, i)

            @pl.when((m >= 23) & (m < 31))
            def _():
                contract(2, m - 23)

            for j, at in ((1, 20), (0, 26), (2, 31)):
                @pl.when(m == at)
                def _():
                    hand_over(j)

            @pl.when((m == 24) | (m == 30))
            def _():
                spread((30 - m) // 6)

        loop(T_END + 4 * OFF, tick)

    last = NCH - 1
    whole = jnp.zeros((MC, W), F32)
    for i in range(4):
        lhs = jnp.concatenate([xt[last, 8 * i + u] for u in range(8)], axis=1)
        whole = whole + jnp.dot(lhs, tmat[i * 1024:(i + 1) * 1024, :], preferred_element_type=F32)
    accs[last] = whole
    hand_over(last)

    @pl.when(jnp.logical_not(root))
    def _():
        spread(last - 1)

    spread(last)

    for t in range(3):
        for s in range(2):
            @pl.when(kids[t][s] >= 0)
            def _():
                count = FIRST[t + 1] - FIRST[t]
                for kind, region in (
                    (0, ext.at[pl.ds(0, RAW), pl.ds(FIRST[t], count)]),
                    (1, ext.at[0, pl.ds(NB, HALO[t + 1] - HALO[t])]),
                    (2, xt.at[pl.ds(RAW, NCH - RAW), pl.ds(FIRST[t], count)]),
                ):
                    pltpu.make_async_remote_copy(
                        src_ref=region, dst_ref=region, send_sem=send_sem.at[t, s, kind],
                        recv_sem=raw_recv.at[0, 0], device_id={"col": kids[t][s]},
                    ).wait_send()
    def finish(j):
        @pl.when(core != j % 2)
        def _():
            pair_copy(j).wait_send()

        @pl.when(core == j % 2)
        def _():
            def sent(q):
                target, copy = part_copy(j, q)

                @pl.when(target != dom)
                def _():
                    copy.wait_send()

            loop(8, sent)

    loop(NCH, finish)

    def arrived(step):
        source = (chip + step + 1) % 16
        pltpu.make_async_remote_copy(
            src_ref=parts.at[0], dst_ref=parts.at[source],
            send_sem=part_send.at[0, 0], recv_sem=part_recv.at[source],
            device_id={"dom": source * 2 + core},
        ).wait_recv()

    loop(15, arrived)
    total = parts[0]
    for s in range(1, 16):
        total = total + parts[s]
    out_ref[...] = total


def couple(live, index, shared, tmat, mass):
    smem = pl.BlockSpec(memory_space=pltpu.SMEM)
    vmem = pl.BlockSpec(memory_space=pltpu.VMEM)
    anyspace = pl.BlockSpec(memory_space=pl.ANY)
    dma = pltpu.SemaphoreType.DMA
    return pl.pallas_call(
        couple_kernel,
        out_shape=jax.ShapeDtypeStruct((16, W), F32),
        in_specs=[smem, vmem, vmem, anyspace, anyspace],
        out_specs=vmem,
        scratch_shapes=[
            pltpu.VMEM((8, LIST), jnp.int32),
            pltpu.SMEM((8, LIST), jnp.int32),
            pltpu.VMEM((NCH, NB + 4, BS, MC), BF16),
            pltpu.VMEM((NCH, NB, MC, BS), BF16),
            pltpu.VMEM((NPAIR, BS, HALF), BF16),
            pltpu.VMEM((BS, HALF), F32),
            pltpu.VMEM((NB * BS, W), BF16),
            pltpu.VMEM((NS + 1, BS, BS), BF16),
            pltpu.VMEM((W, W), BF16),
            pltpu.VMEM((HALF, HALF), BF16),
            pltpu.VMEM((NCH, 4, BS, MC), BF16),
            pltpu.VMEM((NCH, MC, W), F32),
            pltpu.VMEM((2, MC, W), F32),
            pltpu.VMEM((16, 16, W), F32),
            dma((3,)), dma((2,)), dma((2,)), dma((RAW, NB + 4)), dma((NCH - RAW, NB)), dma((3, 2, 3)),
            dma((2,)), dma((2,)), dma((2, 8)), dma((16,)),
        ],
        compiler_params=pltpu.CompilerParams(
            collective_id=0, has_side_effects=True, vmem_limit_bytes=60 << 20
        ),
        name="couple",
    )(live, index, shared, tmat, mass)


def body(tmat, stored_mass_blocks, block_index, live_block_count, send_rows):
    return couple(live_block_count, block_index, send_rows, tmat, stored_mass_blocks)


def solution(mesh):
    return jax.shard_map(
        body,
        mesh=mesh,
        in_specs=(P("dom", "col"), P("dom", None, None), P("dom", None), P("dom"), P("dom", None)),
        out_specs=P("dom", "col"),
        check_vma=False,
    )
```

```python
import functools

import jax
import jax.numpy as jnp
from jax import lax
from jax.experimental import pallas as pl
from jax.experimental.pallas import tpu as pltpu
from jax.sharding import PartitionSpec as P

F32 = jnp.float32
BF16 = jnp.bfloat16
BS = 128
W = 512
NB = 32
NS = 256
NPAIR = (NS + NB) // 2
NCH = 4
MC = W // NCH
OFF = 5
PER = 11
RAW = 1
HALF = 256
LIST = 384

TREES = (
    ("00>10", "10>20", "20>21", "21>31", "10>11", "11>01", "20>30"),
    ("00>30", "30>20", "20>10", "30>31", "31>21", "21>11", "31>01"),
    ("00>01", "01>11", "11>21", "21>20", "01>31", "31>30", "11>10"),
)
FIRST = (0, 11, 22, 32)
HALO = (0, 2, 3, 4)
T_HALO = RAW * PER
T_MASS = T_HALO + 2
T_END = T_MASS + (NCH - RAW) * PER


def column_of(node):
    x, y = int(node[0]), int(node[1])
    return (x + 3) % 4 * 2 + 1 - y


def tree_tables():
    tables = []
    for edges in TREES:
        kids = [[-1, -1] for _ in range(8)]
        depth = [0] * 8
        for edge in edges:
            a, b = (column_of(n) for n in edge.split(">"))
            depth[b] = depth[a] + 1
            kids[a][0 if kids[a][0] < 0 else 1] = b
        tables.append((depth, [k[0] for k in kids], [k[1] for k in kids]))
    return tables


def pick(values, index):
    out = jnp.int32(values[0])
    for i, v in enumerate(values[1:], 1):
        out = jnp.where(index == i, jnp.int32(v), out)
    return out


def couple_kernel(
    live_ref, index_ref, shared_ref, tmat_hbm, mass_hbm, out_ref,
    order_v, order, ext, xt, steps, acc, tmat, mass, perm, eye, lists, accs, pairbuf, parts,
    load_sem, halo_send, halo_recv, raw_recv, x_recv, send_sem,
    pair_send, pair_recv, part_send, part_recv,
):
    col = lax.axis_index("col")
    dom = lax.axis_index("dom")
    core, zed, yhi = dom % 2, dom // 2 % 8, dom // 16
    chip = yhi * 8 + zed
    sibling = dom + 1 - 2 * core
    root = col == 7
    tables = tree_tables()
    depths = [pick(t[0], col) for t in tables]
    kids = [[pick(t[1], col), pick(t[2], col)] for t in tables]

    def loop(n, f):
        def step(i, _):
            f(i)
            return 0

        lax.fori_loop(0, n, step, 0)

    tmat_load = pltpu.make_async_copy(tmat_hbm, tmat, load_sem.at[0])
    tmat_load.start()
    mass_load = pltpu.make_async_copy(mass_hbm, mass.at[pl.ds(0, NS)], load_sem.at[1])

    barrier = pltpu.get_barrier_semaphore()
    xpos, ylo = col // 2, col % 2
    for near in ((xpos + 1) % 4 * 2 + ylo, (xpos + 3) % 4 * 2 + ylo, xpos * 2 + 1 - ylo):
        pl.semaphore_signal(barrier, inc=1, device_id={"col": near})
    for near in ((dom + 1) % 32, (dom + 31) % 32):
        pl.semaphore_signal(barrier, inc=1, device_id={"dom": near})

    def greet(step):
        far = (chip + step + 1) % 16
        pl.semaphore_signal(barrier, inc=1, device_id={"dom": far * 2 + core})

    loop(15, greet)

    mass[NS] = jnp.zeros((BS, BS), BF16)
    eye[...] = (
        lax.broadcasted_iota(jnp.int32, (HALF, HALF), 0) == lax.broadcasted_iota(jnp.int32, (HALF, HALF), 1)
    ).astype(BF16)

    def piece(kind, t, j, b, target, s):
        ref = ext.at[j, b] if kind < 2 else xt.at[RAW + j, b]
        sem = raw_recv.at[j, b] if kind < 2 else x_recv.at[j, b]
        return pltpu.make_async_remote_copy(
            src_ref=ref, dst_ref=ref, send_sem=send_sem.at[t, s, kind], recv_sem=sem,
            device_id={"col": target},
        )

    def plan():
        I32 = jnp.int32

        def iota(shape, axis):
            return lax.broadcasted_iota(I32, shape, axis)

        def add(condition, values, axis):
            return jnp.sum(jnp.where(condition, values, 0), axis=axis, keepdims=True)

        down = iota((NS, 1), 0)
        key = jnp.where(down < live_ref[0], index_ref[:, 0:1], NB)
        key_lane = add(iota((NS, NS), 0) == iota((NS, NS), 1), key, 0)
        before = add((key == key_lane) & (iota((NS, NS), 1) < iota((NS, NS), 0)), 1, 1)
        pairs_lane = (add(key == iota((NS, BS), 1), 1, 0) + 1) // 2
        pairs = (add(iota((NB, NS), 0) == key_lane, 1, 1) + 1) // 2
        base = add(iota((NS, BS), 1) < key, pairs_lane, 1)
        start = add(iota((NB, BS), 1) < iota((NB, BS), 0), pairs_lane, 1)
        place = jnp.where(key < NB, 2 * base + before, LIST)
        hit = place == iota((NS, LIST), 1)
        order_v[...] = jnp.zeros_like(order_v)
        order_v[0:1] = jnp.clip(NS - add(hit, NS - down, 0), 0, NS)
        order_v[1:2] = jnp.clip(add(hit, index_ref[:, 1:2], 0), 0, NB + 3)
        order_v[2:3] = 1 - add(start == iota((NB, LIST), 1), 1, 0)
        order_v[3:4] = jnp.clip(add(iota((NB, LIST), 0) <= iota((NB, LIST), 1), pairs, 0) - 1, 0, NPAIR - 1)
        copy = pltpu.make_async_copy(order_v, order, load_sem.at[2])
        copy.start()
        copy.wait()

    def mass_step(n, first, unr, k):
        prods = []
        for u in range(unr):
            q = k * unr + u
            blocks = jnp.concatenate([mass[order[0, 2 * q]], mass[order[0, 2 * q + 1]]], axis=1)
            rows = jnp.concatenate(
                [
                    jnp.concatenate([ext[first + v, order[1, 2 * q + w]] for v in range(n)], axis=1)
                    for w in range(2)
                ],
                axis=0,
            )
            prods.append(jnp.dot(blocks, rows, preferred_element_type=F32))
        total = acc[:, :n * MC]
        for u in range(unr):
            total = total * order[2, k * unr + u].astype(F32) + prods[u]
            steps[k * unr + u, :, :n * MC] = total.astype(BF16)
        acc[:, :n * MC] = total

    def turned_block(n, r):
        return lax.dot_general(
            eye[:n * MC, :n * MC], steps[order[3, r], :, :n * MC], (((1,), (1,)), ((), ())),
            preferred_element_type=F32,
        ).astype(BF16)

    def turn(n, first, r):
        done = turned_block(n, r)
        for v in range(n):
            xt[first + v, r] = done[v * MC:(v + 1) * MC]

    def contract(j, i):
        lhs = jnp.concatenate([xt[j, 4 * i + u] for u in range(4)], axis=1)
        rhs = tmat[pl.ds(pl.multiple_of(i * 512, 512), 512), :]
        accs[j] += jnp.dot(lhs, rhs, preferred_element_type=F32)

    def contract_wide(j, i):
        lhs = jnp.concatenate([xt[j, 8 * i + u] for u in range(8)], axis=1)
        rhs = tmat[pl.ds(pl.multiple_of(i * 1024, 1024), 1024), :]
        accs[j] += jnp.dot(lhs, rhs, preferred_element_type=F32)

    def pair_copy(j):
        return pltpu.make_async_remote_copy(
            src_ref=accs.at[j], dst_ref=pairbuf.at[j // 2],
            send_sem=pair_send.at[j // 2], recv_sem=pair_recv.at[j // 2],
            device_id={"dom": sibling},
        )

    def part_copy(j, q):
        target = q // 4 * 16 + (q % 4 * 2 + j // 2) * 2 + core
        return target, pltpu.make_async_remote_copy(
            src_ref=accs.at[j, pl.ds(pl.multiple_of(q * 16, 16), 16)], dst_ref=parts.at[chip],
            send_sem=part_send.at[j // 2, q], recv_sem=part_recv.at[chip],
            device_id={"dom": target},
        )

    def hand_over(j):
        @pl.when(core != j % 2)
        def _():
            pair_copy(j).start()

    def spread(j):
        @pl.when(core == j % 2)
        def _():
            pair_copy(j).wait_recv()
            accs[j] += pairbuf[j // 2]

            def send_part(q):
                target, copy = part_copy(j, q)

                @pl.when(target != dom)
                def _():
                    copy.start()

                @pl.when(target == dom)
                def _():
                    parts[chip] = accs[j, pl.ds(pl.multiple_of(q * 16, 16), 16)]

            loop(8, send_part)

    def from_root(kind, t, j, b):
        piece(kind, t, j, b, pick(tables[t][1], jnp.int32(7)), 0).start()

    @pl.when(root)
    def _():
        mode = lax.broadcasted_iota(jnp.int32, (W, W), 0)
        place = lax.broadcasted_iota(jnp.int32, (W, W), 1)
        wanted = (place // 16 % 8) * 64 + (place // MC) * 16 + place % 16
        perm[...] = (mode == wanted).astype(BF16)
        plan()
        tmat_load.wait()
        mass_load.start()

        square = (2 * BS, 2 * BS)
        diagonal = lax.broadcasted_iota(jnp.int32, square, 0) == lax.broadcasted_iota(jnp.int32, square, 1)
        wanted_rows = [
            jnp.sum(jnp.where(diagonal, shared_ref[h:h + 1], 0), axis=1, keepdims=True) for h in range(2)
        ]
        idx = jnp.concatenate(wanted_rows, axis=0)
        accs[...] = jnp.zeros_like(accs)

        def gather(k):
            lane = lax.broadcasted_iota(jnp.int32, (4 * BS, 8 * BS), 1)
            picks = (idx == lane + k * 8 * BS).astype(BF16)
            rows = tmat[pl.ds(pl.multiple_of(k * 8 * BS, 8 * BS), 8 * BS), :]
            got = jnp.dot(picks, rows, preferred_element_type=F32)
            for h in range(4):
                accs[h] += got[h * BS:(h + 1) * BS]

        loop(NB // 8, gather)
        got = jnp.concatenate([accs[h].astype(BF16) for h in range(4)], axis=0)
        got = jnp.dot(got, perm[...], preferred_element_type=F32).astype(BF16)
        for h in range(4):
            for j in range(NCH):
                lists[j, h] = got[h * BS:(h + 1) * BS, j * MC:(j + 1) * MC]

        pl.semaphore_wait(barrier, 20)
        def to_upper():
            return pltpu.make_async_remote_copy(
                src_ref=lists.at[:, pl.ds(2, 2)], dst_ref=ext.at[:, pl.ds(NB, 2)],
                send_sem=halo_send.at[0], recv_sem=halo_recv.at[0], device_id={"dom": (dom + 1) % 32},
            )

        def to_lower():
            return pltpu.make_async_remote_copy(
                src_ref=lists.at[:, pl.ds(0, 2)], dst_ref=ext.at[:, pl.ds(NB + 2, 2)],
                send_sem=halo_send.at[1], recv_sem=halo_recv.at[1], device_id={"dom": (dom + 31) % 32},
            )

        @pl.when(dom < 31)
        def _():
            to_upper().start()

        @pl.when(dom > 0)
        def _():
            to_lower().start()

        def trio(i, make, store):
            blocks = [FIRST[0] + i, FIRST[1] + i, jnp.minimum(FIRST[2] + i, NB - 1)]
            made = make(blocks)
            for t in range(3):
                @pl.when(i < FIRST[t + 1] - FIRST[t])
                def _():
                    store(t, blocks[t], made[t])

        def send_raw(i):
            def make(blocks):
                rows = jnp.concatenate([tmat[pl.ds(pl.multiple_of(b * BS, BS), BS), :] for b in blocks], axis=0)
                turned = jnp.dot(rows, perm[...], preferred_element_type=F32).astype(BF16)
                return [turned[t * BS:(t + 1) * BS] for t in range(3)]

            def store(t, b, turned):
                for j in range(NCH):
                    ext[j, b] = turned[:, j * MC:(j + 1) * MC]
                from_root(0, t, 0, b)

            trio(i, make, store)

        loop(PER, send_raw)
        mass_load.wait()

        @pl.when(dom > 0)
        def _():
            to_upper().wait_recv()

        @pl.when(dom == 0)
        def _():
            ext[:, NB:NB + 2] = jnp.zeros((NCH, 2, BS, MC), BF16)

        @pl.when(dom < 31)
        def _():
            to_lower().wait_recv()

        @pl.when(dom == 31)
        def _():
            ext[:, NB + 2:NB + 4] = jnp.zeros((NCH, 2, BS, MC), BF16)

        for t in range(3):
            for h in range(HALO[t], HALO[t + 1]):
                from_root(1, t, h // 4, NB + h % 4)

        def product(n, first, unr):
            acc[...] = jnp.zeros_like(acc)
            loop(NPAIR // unr, functools.partial(mass_step, n, first, unr))

        def send_mass(n, first, j, i):
            def store(t, b, done):
                for v in range(n):
                    xt[first + v, b] = done[v * MC:(v + 1) * MC]
                from_root(2, t, j, b)

            trio(i, lambda blocks: [turned_block(n, b) for b in blocks], store)

        def send_last(i):
            for t in range(3):
                @pl.when(i < FIRST[t + 1] - FIRST[t])
                def _():
                    from_root(2, t, 2, FIRST[t] + i)

        product(1, 1, 24)
        loop(PER, functools.partial(send_mass, 1, 1, 0))
        product(2, 2, 12)
        loop(PER, functools.partial(send_mass, 2, 2, 1))
        loop(PER, send_last)
        product(1, 0, 16)

        def turn_four(i):
            for u in range(4):
                turn(1, 0, 4 * i + u)

        loop(NB // 4, turn_four)
        accs[...] = jnp.zeros_like(accs)

        def reduce_chunk(j):
            loop(4, functools.partial(contract_wide, j))
            hand_over(j)

            @pl.when(j > 0)
            def _():
                spread(j - 1)

        loop(NCH - 1, reduce_chunk)
        spread(NCH - 2)

        @pl.when(dom < 31)
        def _():
            to_upper().wait_send()

        @pl.when(dom > 0)
        def _():
            to_lower().wait_send()

    def relay(kind, t, j, b):
        piece(kind, t, j, b, kids[t][0], 0).wait_recv()
        for s in range(2):
            @pl.when(kids[t][s] >= 0)
            def _():
                piece(kind, t, j, b, kids[t][s], s).start()

    @pl.when(jnp.logical_not(root))
    def _():
        accs[...] = jnp.zeros_like(accs)
        acc[...] = jnp.zeros_like(acc)
        tmat_load.wait()
        mass_load.start()
        plan()
        pl.semaphore_wait(barrier, 20)

        def tick(k):
            for t in range(3):
                p = k - OFF * depths[t]
                count = FIRST[t + 1] - FIRST[t]

                @pl.when((p >= 0) & (p < T_HALO) & (p % PER < count))
                def _():
                    relay(0, t, p // PER, FIRST[t] + p % PER)

                h = HALO[t] + p - T_HALO

                @pl.when((p >= T_HALO) & (h < HALO[t + 1]))
                def _():
                    relay(1, t, h // 4, NB + h % 4)

                x = p - T_MASS

                @pl.when((x >= 0) & (p < T_END) & (x % PER < count))
                def _():
                    relay(2, t, x // PER, FIRST[t] + x % PER)

            m = k - (T_MASS + 4 * OFF)

            @pl.when(m == 0)
            def _():
                mass_load.wait()

            @pl.when((m >= 0) & (m < 18))
            def _():
                mass_step(1, 0, 8, m)

            @pl.when((m >= 12) & (m < 16))
            def _():
                contract_wide(1, m - 12)

            @pl.when((m >= 18) & (m < 26))
            def _():
                i = m - 18
                for u in range(4):
                    turn(1, 0, 4 * i + u)
                contract(0, i)

            @pl.when((m >= 26) & (m < 30))
            def _():
                contract_wide(2, m - 26)

            for j, at in ((1, 20), (0, 26), (2, 31)):
                @pl.when(m == at)
                def _():
                    hand_over(j)

            @pl.when((m == 24) | (m == 30))
            def _():
                spread((30 - m) // 6)

        loop(T_END + 4 * OFF, tick)

    last = NCH - 1
    whole = jnp.zeros((MC, W), F32)
    for i in range(4):
        lhs = jnp.concatenate([xt[last, 8 * i + u] for u in range(8)], axis=1)
        whole = whole + jnp.dot(lhs, tmat[i * 1024:(i + 1) * 1024, :], preferred_element_type=F32)
    accs[last] = whole
    hand_over(last)

    @pl.when(jnp.logical_not(root))
    def _():
        spread(last - 1)

    spread(last)

    for t in range(3):
        for s in range(2):
            @pl.when(kids[t][s] >= 0)
            def _():
                count = FIRST[t + 1] - FIRST[t]
                for kind, region in (
                    (0, ext.at[pl.ds(0, RAW), pl.ds(FIRST[t], count)]),
                    (1, ext.at[0, pl.ds(NB, HALO[t + 1] - HALO[t])]),
                    (2, xt.at[pl.ds(RAW, NCH - RAW), pl.ds(FIRST[t], count)]),
                ):
                    pltpu.make_async_remote_copy(
                        src_ref=region, dst_ref=region, send_sem=send_sem.at[t, s, kind],
                        recv_sem=raw_recv.at[0, 0], device_id={"col": kids[t][s]},
                    ).wait_send()
    def finish(j):
        @pl.when(core != j % 2)
        def _():
            pair_copy(j).wait_send()

        @pl.when(core == j % 2)
        def _():
            def sent(q):
                target, copy = part_copy(j, q)

                @pl.when(target != dom)
                def _():
                    copy.wait_send()

            loop(8, sent)

    loop(NCH, finish)

    def arrived(step):
        source = (chip + step + 1) % 16
        pltpu.make_async_remote_copy(
            src_ref=parts.at[0], dst_ref=parts.at[source],
            send_sem=part_send.at[0, 0], recv_sem=part_recv.at[source],
            device_id={"dom": source * 2 + core},
        ).wait_recv()

    loop(15, arrived)
    total = parts[0]
    for s in range(1, 16):
        total = total + parts[s]
    out_ref[...] = total


def couple(live, index, shared, tmat, mass):
    smem = pl.BlockSpec(memory_space=pltpu.SMEM)
    vmem = pl.BlockSpec(memory_space=pltpu.VMEM)
    anyspace = pl.BlockSpec(memory_space=pl.ANY)
    dma = pltpu.SemaphoreType.DMA
    return pl.pallas_call(
        couple_kernel,
        out_shape=jax.ShapeDtypeStruct((16, W), F32),
        in_specs=[smem, vmem, vmem, anyspace, anyspace],
        out_specs=vmem,
        scratch_shapes=[
            pltpu.VMEM((8, LIST), jnp.int32),
            pltpu.SMEM((8, LIST), jnp.int32),
            pltpu.VMEM((NCH, NB + 4, BS, MC), BF16),
            pltpu.VMEM((NCH, NB, MC, BS), BF16),
            pltpu.VMEM((NPAIR, BS, HALF), BF16),
            pltpu.VMEM((BS, HALF), F32),
            pltpu.VMEM((NB * BS, W), BF16),
            pltpu.VMEM((NS + 1, BS, BS), BF16),
            pltpu.VMEM((W, W), BF16),
            pltpu.VMEM((HALF, HALF), BF16),
            pltpu.VMEM((NCH, 4, BS, MC), BF16),
            pltpu.VMEM((NCH, MC, W), F32),
            pltpu.VMEM((2, MC, W), F32),
            pltpu.VMEM((16, 16, W), F32),
            dma((3,)), dma((2,)), dma((2,)), dma((RAW, NB + 4)), dma((NCH - RAW, NB)), dma((3, 2, 3)),
            dma((2,)), dma((2,)), dma((2, 8)), dma((16,)),
        ],
        compiler_params=pltpu.CompilerParams(
            collective_id=0, has_side_effects=True, vmem_limit_bytes=60 << 20
        ),
        name="couple",
    )(live, index, shared, tmat, mass)


def body(tmat, stored_mass_blocks, block_index, live_block_count, send_rows):
    return couple(live_block_count, block_index, send_rows, tmat, stored_mass_blocks)


def solution(mesh):
    return jax.shard_map(
        body,
        mesh=mesh,
        in_specs=(P("dom", "col"), P("dom", None, None), P("dom", None), P("dom"), P("dom", None)),
        out_specs=P("dom", "col"),
        check_vma=False,
    )
```
